32 devices in a mesh: outer: 4 (over y, core), dev: 8 (over z, x).
Axes of the slice: x: 2, y: 2, z: 4, core: 2. Of those that a mesh axis runs over, the one named last changes fastest.
Arguments:
- gradients: bfloat16 [4, 8, 128, 20480], P('outer', 'dev'), may hold values from -6 to 6
- momentum: float32 [4, 128, 20480], P('outer', None, 'dev'), may hold values from -4 to 4
- chosen: int32 [4, 2, 320, 32], P(None, None, 'dev'), may hold values from 0 to 4095, as said below
Outputs:
- momentum_out: float32 [4, 128, 20480], P('outer', None, 'dev')
- update: float32 [128, 20480], P(None, 'dev')
The draws below stay inside these ranges and needn't reach their ends.
Inputs may be any that keep to these rules, and one draw needn't show every extreme that they name: `chosen`: within each block the 32 positions are distinct; an entry i stands for row i // 64 and column i % 64 of the block's table.
All inputs are finite; a program needn't handle non-finite values.
Results may differ from the reference program's by a relative error of at most 0.0003.
Values sent between devices are 32-bit elements; how exact they have to be, the bound alone decides.
No kernel may reach another device: no remote copies, remote signals or barrier semaphores. Data moves between devices by JAX's collectives and lax.ppermute only.
A program may use at most 128 MiB of HBM per device.

```python
import jax
import jax.numpy as jnp
from jax import lax

FF = 20480
GROUP = 64
K = 32
ROWS = 128
CR = 2
CC = 320
N_OUTER = 4
N_DEV = 8


def draw_chosen(key, part):
    cells = GROUP * GROUP
    scores = jax.random.randint(key, (N_OUTER, ROWS // GROUP, FF // GROUP, cells), 0, 262144)
    scores = scores * cells + jnp.arange(cells, dtype=jnp.int32)
    unused, picks = lax.top_k(scores, K)
    return picks.astype(jnp.int32)


def spiked(result, rng, source, target, shards_of, factor):
    owner, partner = [(jnp.arange(result.shape[dim]) // (result.shape[dim] // shards_of)).reshape([-1 if axis == dim else 1 for axis in range(result.ndim)]) for dim in (source, target)]
    chosen = jax.random.permutation(rng, shards_of)[partner]
    strong = (owner == chosen) | (owner == (partner + shards_of // 2) % shards_of)
    return jnp.where(strong, factor * result, result)


def shard_levels(own_key, dims, pieces, least, top_value):
    def one(axis_at, shards_of):
        steps = jax.random.uniform(jax.random.fold_in(jax.random.fold_in(own_key, 6), axis_at), (shards_of,), jnp.float32, least / len(pieces), top_value / len(pieces))
        return jnp.repeat(jnp.exp(steps), dims[axis_at] // shards_of).reshape((-1,) + (1,) * (len(dims) - axis_at - 1))

    gain = one(*pieces[0])
    for cut in pieces[1:]:
        gain = gain * one(*cut)
    return gain


def gaussian(stream_key, dims, width, limit, cuts=(), kind=jnp.bfloat16):
    array = width * jax.random.normal(stream_key, dims, jnp.float32)
    if cuts:
        array = array * shard_levels(stream_key, dims, cuts, -0.22, 0.18)
    return jnp.clip(array, -limit, limit).astype(kind)


def noise_with(stream_key, dims, width, limit, cuts, heavy, kind=jnp.bfloat16):
    values = width * jax.random.normal(stream_key, dims, jnp.float32)
    if cuts:
        values = values * shard_levels(stream_key, dims, cuts, -0.22, 0.18)
    return jnp.clip(spiked(values, jax.random.fold_in(stream_key, 3), *heavy), -limit, limit).astype(kind)


def setup_inputs(seed: int = 0) -> dict:
    splits = jax.random.split(jax.random.key(seed), 4)
    gradients = noise_with(splits[0], (N_OUTER, N_DEV, ROWS, FF), 1.0, 6.0, ((0, 4), (1, 8)), (1, 3, 8, 2.0))
    momentum = gaussian(splits[1], (N_OUTER, ROWS, FF), 0.5, 4.0, ((0, 4), (2, 8)), jnp.float32)
    chosen = draw_chosen(jax.random.fold_in(splits[3], 71), 0)
    return dict(gradients=gradients, momentum=momentum, chosen=chosen)


decay_rate = 0.999
tiny_eps = 1e-06

def cosine_basis(size):
    freq = jnp.arange(size, dtype=jnp.float32)[:, None]
    place = jnp.arange(size, dtype=jnp.float32)[None, :]
    weight = jnp.where(freq == 0, jnp.sqrt(jnp.float32(1.0 / size)), jnp.sqrt(jnp.float32(2.0 / size)))
    return (weight * jnp.cos(jnp.pi * (2.0 * place + 1.0) * freq / (2.0 * size))).astype(jnp.float32)

def to_spectrum(spatial, basis):
    side = basis.shape[0]
    row_all, col_all = spatial.shape
    blocks = spatial.reshape(row_all // side, side, col_all // side, side)
    out = jnp.einsum('ij,rjsk,lk->sril', basis, blocks, basis, precision=lax.Precision.HIGHEST)
    return out.reshape(col_all // side, row_all // side, side * side)

def from_spectrum(spectrum, basis):
    side = basis.shape[0]
    col_blocks, row_blocks = (spectrum.shape[0], spectrum.shape[1])
    blocks = spectrum.reshape(col_blocks, row_blocks, side, side)
    out = jnp.einsum('ij,sril,lk->rjsk', basis, blocks, basis, precision=lax.Precision.HIGHEST)
    return out.reshape(row_blocks * side, col_blocks * side)

def normalise(decoded, side):
    row_all, col_all = decoded.shape
    blocks = decoded.reshape(row_all // side, side, col_all // side, side)
    square_mean = lax.optimization_barrier(jnp.mean(blocks * blocks, axis=(1, 3), keepdims=True))
    return (blocks / jnp.sqrt(square_mean + tiny_eps)).reshape(row_all, col_all)

def reference(gradients, momentum, chosen):
    basis = cosine_basis(GROUP)
    summed = lax.optimization_barrier(jnp.sum(gradients, axis=1, dtype=jnp.float32))
    blend = decay_rate * momentum + summed / N_DEV
    spectrum = jax.vmap(lambda field: to_spectrum(field, basis))(blend)
    picks = jnp.transpose(chosen, (0, 2, 1, 3)).astype(jnp.int32)
    picked = jnp.take_along_axis(spectrum, picks, axis=3)
    pod_ids = jnp.arange(N_OUTER).astype(jnp.int32)[:, None, None, None]
    col_ids = jnp.arange(CC).astype(jnp.int32)[None, :, None, None]
    row_ids = jnp.arange(CR).astype(jnp.int32)[None, None, :, None]
    own_table = jnp.zeros_like(spectrum).at[pod_ids, col_ids, row_ids, picks].set(picked)
    momentum_out = blend - jax.vmap(lambda table: from_spectrum(table, basis))(own_table)
    pod_sum = lax.optimization_barrier(jnp.sum(own_table, axis=0))
    update = normalise(from_spectrum(pod_sum, basis), GROUP)
    return (momentum_out, update)
```

```python
import functools

import jax
import jax.numpy as jnp
import numpy as np
from jax import lax
from jax.experimental import pallas as pl
from jax.experimental.pallas import tpu as pltpu
from jax.sharding import PartitionSpec as P

GROUP = 64
LANES = 128

decay_rate = 0.999
tiny_eps = 1e-06


VMEM_LIMIT = 16 << 20
bf16 = jnp.bfloat16
f32 = jnp.float32


def cosine_basis(size):
    freq = np.arange(size, dtype=np.float64)[:, None]
    place = np.arange(size, dtype=np.float64)[None, :]
    weight = np.where(freq == 0, np.sqrt(1.0 / size), np.sqrt(2.0 / size))
    return (weight * np.cos(np.pi * (2.0 * place + 1.0) * freq / (2.0 * size))).astype(np.float32)


def halves_of(table):
    high = table.astype(bf16)
    return np.stack([high, (table - high.astype(np.float32)).astype(bf16)])


def split(x):
    high = x.astype(bf16)
    return high, (x - high.astype(f32)).astype(bf16)


def mm(a, b):
    return jnp.dot(a, b, preferred_element_type=f32)


def mm_nt(a, b):
    return lax.dot_general(a, b, (((1,), (1,)), ((), ())), preferred_element_type=f32)


def mm3(x, table):
    high, low = split(x)
    return mm(high, table[0]) + (mm(low, table[0]) + mm(high, table[1]))


def selectors(idx, kept, side):
    count = idx.shape[1]
    per = LANES // kept
    lane = lax.broadcasted_iota(jnp.int32, (1, count), 1)
    cell = lax.rem(lane, LANES) // kept
    row = idx // side
    col = cell * side + lax.rem(idx, side)
    at_row = lax.broadcasted_iota(jnp.int32, (side, count), 0) == row
    at_col = lax.broadcasted_iota(jnp.int32, (per * side, count), 0) == col
    return (jnp.where(at_row, 1.0, 0.0).astype(bf16), jnp.where(at_col, 1.0, 0.0).astype(bf16))


def basis_rows(tall, at_row):
    return mm(tall[0], at_row) + mm(tall[1], at_row)


def picks_of(x, idx, wide_t, tall, kept, side):
    at_row, at_col = selectors(idx, kept, side)
    high, low = split(mm3(x, wide_t))
    cols = mm(high, at_col) + mm(low, at_col)
    return jnp.sum(cols * basis_rows(tall, at_row), axis=0, keepdims=True)


def spatial_of(values, idx, wide, tall, kept, side):
    at_row, at_col = selectors(idx, kept, side)
    high, low = split(basis_rows(tall, at_row) * values)
    return mm3(mm_nt(high, at_col) + mm_nt(low, at_col), wide)


def own_kernel(kept, side, members, where_ref, grad_ref, mom_ref, idx_ref, wide_t_ref, tall_ref, x_ref, v_ref):
    q = pl.program_id(0)
    for r in range(idx_ref.shape[0]):
        rows = pl.ds(r * side, side)
        x = decay_rate * mom_ref[rows, :] + grad_ref[rows, :].astype(f32) / members
        x_ref[rows, :] = x
        v_ref[r, pl.ds(q, 1), :] = picks_of(x, idx_ref[r, pl.ds(q, 1), :], wide_t_ref, tall_ref, kept, side)


def own_part(grad, mom, idx, block, wide_t, tall, kept, side, members, first, count):
    rows, span = mom.shape[0], wide_t.shape[1]
    whole = lambda a: pl.BlockSpec(a.shape, lambda q, w: (0,) * a.ndim)
    part = pl.BlockSpec((rows, span), lambda q, w: (0, q))
    v_shape = jax.ShapeDtypeStruct(idx.shape, f32)
    return pl.pallas_call(
        functools.partial(own_kernel, kept, side, members),
        out_shape=(jax.ShapeDtypeStruct((rows, count * span), f32), v_shape),
        grid_spec=pltpu.PrefetchScalarGridSpec(
            num_scalar_prefetch=1,
            grid=(count,),
            in_specs=[
                pl.BlockSpec((rows, span), lambda q, w: (0, w[0] + first + q)),
                pl.BlockSpec((rows, span), lambda q, w: (0, first + q)),
                whole(idx),
                whole(wide_t),
                whole(tall),
            ],
            out_specs=(part, whole(v_shape)),
        ),
        compiler_params=pltpu.CompilerParams(vmem_limit_bytes=VMEM_LIMIT),
        cost_estimate=pl.CostEstimate(
            flops=rows * span * span * count * 10, bytes_accessed=rows * span * count * 10, transcendentals=0
        ),
    )(block, grad, mom, idx, wide_t, tall)


def send_kernel(kept, side, members, x_ref, idx_ref, wide_t_ref, tall_ref, v_ref):
    span = wide_t_ref.shape[1]
    for q in range(idx_ref.shape[0]):
        x = x_ref[:, pl.ds(q * span, span)]
        v_ref[pl.ds(q, 1), :] = picks_of(x, idx_ref[pl.ds(q, 1), :], wide_t_ref, tall_ref, kept, side) / members


def send_part(x, idx, wide_t, tall, kept, side, members):
    vmem = pl.BlockSpec(memory_space=pltpu.VMEM)
    return pl.pallas_call(
        functools.partial(send_kernel, kept, side, members),
        out_shape=jax.ShapeDtypeStruct(idx.shape, f32),
        in_specs=[vmem] * 4,
        out_specs=vmem,
        compiler_params=pltpu.CompilerParams(vmem_limit_bytes=VMEM_LIMIT),
        cost_estimate=pl.CostEstimate(
            flops=x.shape[0] * x.shape[1] * 2000, bytes_accessed=x.size * 4, transcendentals=0
        ),
    )(pltpu.with_memory_space_constraint(x, pltpu.VMEM), idx, wide_t, tall)


def decode_kernel(kept, side, pod_ref, v_ref, idx_ref, x_ref, wide_ref, tall_ref, same_ref, *refs):
    update_ref, rest_ref = refs[-2:]
    q = pl.program_id(0)
    pods, blocks = idx_ref.shape[:2]
    pod = pod_ref[0]
    for r in range(blocks):
        rows = pl.ds(r * side, side)
        own = spatial_of(
            v_ref[pod, r, pl.ds(q, 1), :], idx_ref[pod, r, pl.ds(q, 1), :], wide_ref, tall_ref, kept, side
        )
        rest_ref[rows, :] = x_ref[rows, :] - own
        values = jnp.concatenate([v_ref[p, r, pl.ds(q, 1), :] for p in range(pods)], axis=1)
        places = jnp.concatenate([idx_ref[p, r, pl.ds(q, 1), :] for p in range(pods)], axis=1)
        decoded = spatial_of(values, places, wide_ref, tall_ref, kept, side)
        squares = jnp.sum(decoded * decoded, axis=0, keepdims=True) / (side * side)
        high, low = split(jnp.broadcast_to(squares, (8, squares.shape[1])))
        mean = mm(high, same_ref[...]) + mm(low, same_ref[...])
        update_ref[rows, :] = decoded / jnp.sqrt(mean[0:1, :] + tiny_eps)


def decode_part(pod, values, idx, x, wide, tall, same, kept, side, columns, first, count, update=None):
    rows, span = x.shape[0], wide.shape[1]
    whole = lambda a: pl.BlockSpec(a.shape, lambda q, w: (0,) * a.ndim)
    part = pl.BlockSpec((rows, span), lambda q, w: (0, q))
    operands = [values, idx, x, wide, tall, same]
    specs = [whole(values), whole(idx), part, whole(wide), whole(tall), whole(same)]
    alias = {}
    if update is not None:
        alias = {1 + len(operands): 0}
        operands.append(update)
        specs.append(pl.BlockSpec(memory_space=pl.ANY))
    return pl.pallas_call(
        functools.partial(decode_kernel, kept, side),
        out_shape=(jax.ShapeDtypeStruct((rows, columns), f32), jax.ShapeDtypeStruct(x.shape, f32)),
        grid_spec=pltpu.PrefetchScalarGridSpec(
            num_scalar_prefetch=1,
            grid=(count,),
            in_specs=specs,
            out_specs=(pl.BlockSpec((rows, span), lambda q, w: (0, first + q)), part),
        ),
        input_output_aliases=alias,
        compiler_params=pltpu.CompilerParams(vmem_limit_bytes=VMEM_LIMIT),
        cost_estimate=pl.CostEstimate(
            flops=rows * span * span * count * 20, bytes_accessed=rows * span * count * 12, transcendentals=0
        ),
    )(pod, *operands)


def ring_order(n):
    return [2 * q if q < n // 2 else 2 * n - 1 - 2 * q for q in range(n)]


def ring_at(q, n):
    return jnp.where(q < n // 2, 2 * q, 2 * n - 1 - 2 * q)


def local(gradients, momentum, chosen, pods, members):
    kept = chosen.shape[3]
    side = GROUP
    per = LANES // kept
    span = per * side
    grad, mom = gradients[0, 0], momentum[0]
    rows, width = mom.shape
    blocks = rows // side
    pod = lax.axis_index("outer")
    me = lax.axis_index("dev")

    basis = cosine_basis(side)
    many = np.kron(np.eye(per, dtype=np.float32), basis)
    wide, wide_t, tall = (jnp.asarray(halves_of(t)) for t in (many, many.T, basis.T))
    same = jnp.asarray(np.kron(np.eye(per), np.ones((side, side))).astype(bf16))
    where = functools.partial(dict, kept=kept, side=side)

    chunks = 2
    if blocks != 2 or members % 2 or width % (chunks * span):
        summed = lax.psum_scatter(grad.astype(f32), "dev", scatter_dimension=1, tiled=True)
        pad = -width % span
        mom, summed = (jnp.pad(a, ((0, 0), (0, pad))) for a in (mom, summed))
        places = jnp.pad(chosen, ((0, 0), (0, 0), (0, pad // side), (0, 0)))
        count = (width + pad) // span
        places = places.reshape(pods, blocks, count, LANES)
        own_places = lax.dynamic_index_in_dim(places, pod, 0, keepdims=False)
        zero = jnp.zeros((1,), jnp.int32)
        x, v = own_part(summed, mom, own_places, zero, wide_t, tall, members=members, first=0, count=count, **where())
        every = lax.all_gather(v, "outer")
        update, rest = decode_part(
            pod[None], every, places, x, wide, tall, same, columns=width + pad, first=0, count=count, **where()
        )
        return rest[None, :, :width], update[:, :width]

    count = width // span
    each = count // chunks
    piece_cols = width // chunks
    places = chosen.reshape(pods, blocks, count, LANES)
    own_places = lax.dynamic_index_in_dim(places, pod, 0, keepdims=False)

    ring = ring_order(members)
    clockwise = [(ring[i], ring[(i + 1) % members]) for i in range(members)]
    counter = [(b, a) for a, b in clockwise]
    ways = (clockwise, counter)
    position = jnp.where(me % 2 == 0, me // 2, members - 1 - me // 2)

    def owner(d, s):
        q = position - 1 - s + members if d == 0 else position + 1 + s
        return ring_at(lax.rem(q, members), members)

    def piece(source, d, s, j):
        start = owner(d, s) * width + j * piece_cols
        return lax.dynamic_slice(source, (d * side, start), (side, piece_cols)).astype(f32)

    def tie(*arrays):
        return lax.optimization_barrier(arrays)

    current = [[None] * 2 for _ in range(chunks)]
    for j in range(chunks):
        for d in range(2):
            (grad,) = tie(grad)
            current[j][d] = piece(grad, d, 0, j)

    next_places = [lax.ppermute(own_places[d], "dev", ways[1 - d]) for d in range(2)]
    own = [None] * chunks
    values = [None] * chunks
    update = None
    last = members - 2
    pieces = [[None] * 2 for _ in range(chunks)]
    for s in range(members - 1):
        for j in range(chunks):
            sent = [None] * 2
            for d in range(2):
                if s == last:
                    v = send_part(
                        current[j][d], next_places[d][j * each : (j + 1) * each], wide_t, tall, members=members, **where()
                    )
                    sent[d] = lax.ppermute(v, "dev", ways[d])
                arrived = lax.ppermute(current[j][d], "dev", ways[d])
                if s < last:
                    arrived, source = tie(arrived, grad)
                    current[j][d] = arrived + piece(source, d, s + 1, j)
                else:
                    pieces[j][d] = arrived
            if s == 1:
                x, v = own_part(
                    grad,
                    mom,
                    own_places[:, j * each : (j + 1) * each],
                    me[None] * count,
                    wide_t,
                    tall,
                    members=members,
                    first=j * each,
                    count=each,
                    **where(),
                )
                own[j] = (x, v)
            if s == last:
                values[j] = own[j][1] + jnp.stack(sent)
    outs = []
    for j in range(chunks):
        every = lax.all_gather(values[j], "outer")
        update, rest = decode_part(
            pod[None],
            every,
            places[:, :, j * each : (j + 1) * each],
            own[j][0],
            wide,
            tall,
            same,
            columns=width,
            first=j * each,
            count=each,
            update=update,
            **where(),
        )
        outs.append(rest + jnp.concatenate(pieces[j], axis=0) / members)
    return jnp.concatenate(outs, axis=1)[None], update


def solution(mesh):
    return jax.shard_map(
        functools.partial(local, pods=mesh.shape["outer"], members=mesh.shape["dev"]),
        mesh=mesh,
        in_specs=(
            P("outer", "dev", None, None),
            P("outer", None, "dev"),
            P(None, None, "dev", None),
        ),
        out_specs=(P("outer", None, "dev"), P(None, "dev")),
        check_vma=False,
    )
```

```python
import functools

import jax
import jax.numpy as jnp
import numpy as np
from jax import lax
from jax.experimental import pallas as pl
from jax.experimental.pallas import tpu as pltpu
from jax.sharding import PartitionSpec as P


GROUP = 64
LANES = 128

decay_rate = 0.999
tiny_eps = 1e-06


VMEM_LIMIT = 16 << 20
bf16 = jnp.bfloat16
f32 = jnp.float32


def cosine_basis(size):
    freq = np.arange(size, dtype=np.float64)[:, None]
    place = np.arange(size, dtype=np.float64)[None, :]
    weight = np.where(freq == 0, np.sqrt(1.0 / size), np.sqrt(2.0 / size))
    return (weight * np.cos(np.pi * (2.0 * place + 1.0) * freq / (2.0 * size))).astype(np.float32)


def halves_of(table):
    high = table.astype(bf16)
    return np.stack([high, (table - high.astype(np.float32)).astype(bf16)])


def split(x):
    high = x.astype(bf16)
    return high, (x - high.astype(f32)).astype(bf16)


def mm(a, b):
    return jnp.dot(a, b, preferred_element_type=f32)


def mm3(x, table):
    high, low = split(x)
    return mm(high, table[0]) + (mm(low, table[0]) + mm(high, table[1]))


def log2(n):
    assert n & (n - 1) == 0
    return n.bit_length() - 1


def table_places(idx, kept, side):
    lane = lax.broadcasted_iota(jnp.int32, idx.shape, 1)
    cell = (lane & (LANES - 1)) >> log2(kept)
    return idx >> log2(side), (cell << log2(side)) + (idx & (side - 1))


def one_hot(hit):
    return jnp.where(hit, 1.0, 0.0).astype(bf16)


def basis_rows(row, tall, side):
    at_row = one_hot(lax.broadcasted_iota(jnp.int32, (side, row.shape[1]), 0) == row)
    return mm(tall[0], at_row) + mm(tall[1], at_row)


def picks_of(xs, places, wide_t, tall, kept, side):
    high, low = split(mm3(jnp.concatenate(xs, axis=0), wide_t))
    found = []
    for i, idx in enumerate(places):
        row, col = table_places(idx, kept, side)
        at_col = one_hot(lax.broadcasted_iota(jnp.int32, (high.shape[1], idx.shape[1]), 0) == col)
        at = slice(i * side, (i + 1) * side)
        cols = mm(high[at], at_col) + mm(low[at], at_col)
        found.append(jnp.sum(cols * basis_rows(row, tall, side), axis=0, keepdims=True))
    return found


def in_vmem(a):
    return pltpu.with_memory_space_constraint(a, pltpu.VMEM)


ON_CHIP = pl.BlockSpec(memory_space=pltpu.VMEM)
PARAMS = pltpu.CompilerParams(vmem_limit_bytes=VMEM_LIMIT)


def cost(flops, moved):
    return pl.CostEstimate(flops=flops, bytes_accessed=moved, transcendentals=0)


def own_kernel(kept, side, members, first, mom_ref, *refs):
    *grad_refs, idx_ref, wide_t_ref, tall_ref, x_ref, v_ref = refs
    parts, count = idx_ref.shape[:2]
    span = wide_t_ref.shape[1]
    spots = [(r, q) for r in range(parts) for q in range(count)]
    xs = []
    for r, q in spots:
        rows = pl.ds(r * side, side)
        x = decay_rate * mom_ref[rows, pl.ds(first + q * span, span)]
        x += grad_refs[r][:, pl.ds(q * span, span)].astype(f32) / members
        x_ref[rows, pl.ds(q * span, span)] = x
        xs.append(x)
    places = [idx_ref[r, pl.ds(q, 1), :] for r, q in spots]
    for (r, q), v in zip(spots, picks_of(xs, places, wide_t_ref, tall_ref, kept, side)):
        v_ref[r, pl.ds(q, 1), :] = v


def own_part(mom, terms, idx, wide_t, tall, kept, side, members, first):
    shape = (mom.shape[0], terms[0].shape[1])
    size = shape[0] * shape[1]
    return pl.pallas_call(
        functools.partial(own_kernel, kept, side, members, first),
        out_shape=(pltpu.VMEM(shape, f32), jax.ShapeDtypeStruct(idx.shape, f32)),
        in_specs=[ON_CHIP] * (len(terms) + 4),
        out_specs=(ON_CHIP, ON_CHIP),
        compiler_params=PARAMS,
        cost_estimate=cost(size * wide_t.shape[1] * 10, size * 10),
    )(in_vmem(mom), *[in_vmem(x) for x in terms], idx, wide_t, tall)


def term_kernel(kept, side, members, *refs):
    *x_refs, idx_ref, wide_t_ref, tall_ref, v_ref = refs
    parts, count = idx_ref.shape[:2]
    span = wide_t_ref.shape[1]
    spots = [(r, q) for r in range(parts) for q in range(count)]
    xs = [x_refs[r][:, pl.ds(q * span, span)].astype(f32) for r, q in spots]
    places = [idx_ref[r, pl.ds(q, 1), :] for r, q in spots]
    for (r, q), v in zip(spots, picks_of(xs, places, wide_t_ref, tall_ref, kept, side)):
        v_ref[r, pl.ds(q, 1), :] = v / members


def term_part(terms, idx, wide_t, tall, kept, side, members):
    return pl.pallas_call(
        functools.partial(term_kernel, kept, side, members),
        out_shape=jax.ShapeDtypeStruct(idx.shape, f32),
        in_specs=[ON_CHIP] * (len(terms) + 3),
        out_specs=ON_CHIP,
        compiler_params=PARAMS,
        cost_estimate=cost(idx.size * side * wide_t.shape[1] * 40, idx.size * side * 4),
    )(*[in_vmem(x) for x in terms], idx, wide_t, tall)


def table_kernel(kept, side, idx_ref, tall_ref, rows_ref, cols_ref):
    pods, parts, count = idx_ref.shape[:3]
    span = cols_ref.shape[3]
    for r in range(parts):
        for q in range(count):
            idx = jnp.concatenate([idx_ref[p, r, pl.ds(q, 1), :] for p in range(pods)], axis=1)
            row, col = table_places(idx, kept, side)
            rows_ref[r, q] = basis_rows(row, tall_ref, side)
            tall_col = jnp.transpose(jnp.broadcast_to(col, (LANES, col.shape[1])))
            for c in range(0, span, LANES):
                lane = lax.broadcasted_iota(jnp.int32, tall_col.shape, 1) + c
                cols_ref[r, q, :, pl.ds(c, LANES)] = one_hot(tall_col == lane)


def table_part(idx, tall, kept, side):
    pods, parts, count, lanes = idx.shape
    span = LANES // kept * side
    return pl.pallas_call(
        functools.partial(table_kernel, kept, side),
        out_shape=(
            pltpu.VMEM((parts, count, side, pods * lanes), f32),
            pltpu.VMEM((parts, count, pods * lanes, span), bf16),
        ),
        in_specs=[ON_CHIP] * 2,
        out_specs=(ON_CHIP, ON_CHIP),
        compiler_params=PARAMS,
        cost_estimate=cost(parts * count * side * side * pods * lanes * 4, parts * count * pods * lanes * span * 2),
    )(idx, tall)


def decode_kernel(side, pod_ref, v_ref, rows_ref, cols_ref, x_ref, wide_ref, same_ref, update_ref, rest_ref, table_ref):
    parts, count, _, lanes = rows_ref.shape
    pods, span = v_ref.shape[0], wide_ref.shape[1]
    mine = (lax.broadcasted_iota(jnp.int32, (1, lanes), 1) >> log2(LANES)) == pod_ref[0]
    for r in range(parts):
        for q in range(count):
            v = jnp.concatenate([v_ref[p, r, pl.ds(q, 1), :] for p in range(pods)], axis=1)
            rows = rows_ref[r, q]
            sides = jnp.concatenate([rows * v, rows * jnp.where(mine, v, 0.0)], axis=0)
            high, low = split(sides)
            table_ref[r * count + q] = mm(high, cols_ref[r, q]) + mm(low, cols_ref[r, q])
    table = table_ref[...].reshape(parts * count * 2 * side, span)
    spatial = mm3(table, wide_ref).reshape(parts * count, 2, side, span)
    shared = spatial[:, 0]
    squares = jnp.sum(shared * shared, axis=1) / (side * side)
    high, low = split(squares)
    mean = mm(high, same_ref[...]) + mm(low, same_ref[...])
    scale = 1.0 / jnp.sqrt(mean + tiny_eps)
    for r in range(parts):
        for q in range(count):
            at = (pl.ds(r * side, side), pl.ds(q * span, span))
            b = r * count + q
            update_ref[at] = shared[b] * scale[b : b + 1, :]
            rest_ref[at] = x_ref[at] - spatial[b, 1]


def decode_part(pod, values, rows, cols, x, wide, same, side):
    parts, count = rows.shape[:2]
    return pl.pallas_call(
        functools.partial(decode_kernel, side),
        out_shape=(pltpu.VMEM(x.shape, f32), pltpu.VMEM(x.shape, f32)),
        in_specs=[pl.BlockSpec(memory_space=pltpu.SMEM)] + [ON_CHIP] * 6,
        out_specs=(ON_CHIP, ON_CHIP),
        scratch_shapes=[pltpu.VMEM((parts * count, 2 * side, wide.shape[1]), f32)],
        compiler_params=PARAMS,
        cost_estimate=cost(x.size * wide.shape[1] * 20, x.size * 12),
    )(pod, values, in_vmem(rows), in_vmem(cols), in_vmem(x), wide, same)


def ring_order(n):
    return [2 * q if q < n // 2 else 2 * n - 1 - 2 * q for q in range(n)]


def ring_at(q, n):
    return jnp.where(q < n // 2, 2 * q, 2 * n - 1 - 2 * q)


CHUNKS = 2


def local(gradients, momentum, chosen, pods, members):
    kept = chosen.shape[3]
    side = GROUP
    per = LANES // kept
    span = per * side
    grad, mom = gradients[0, 0], momentum[0]
    rows, width = mom.shape
    blocks = rows // side
    pod = lax.axis_index("outer")
    me = lax.axis_index("dev")

    basis = cosine_basis(side)
    many = np.kron(np.eye(per, dtype=np.float32), basis)
    wide, wide_t, tall = (jnp.asarray(halves_of(t)) for t in (many, many.T, basis.T))
    same = jnp.asarray(np.kron(np.eye(per), np.ones((side, side))).astype(bf16))
    how = dict(kept=kept, side=side)

    chunks = CHUNKS
    if blocks != 2 or members % 2 or width % (chunks * span):
        summed = lax.psum_scatter(grad.astype(f32), "dev", scatter_dimension=1, tiled=True)
        pad = -width % span
        mom, summed = (jnp.pad(a, ((0, 0), (0, pad))) for a in (mom, summed))
        places = jnp.pad(chosen, ((0, 0), (0, 0), (0, pad // side), (0, 0)))
        count = (width + pad) // span
        places = places.reshape(pods, blocks, count, LANES)
        own_places = lax.dynamic_index_in_dim(places, pod, 0, keepdims=False)
        terms = [summed[r * side : (r + 1) * side] for r in range(blocks)]
        x, v = own_part(mom, terms, own_places, wide_t, tall, members=members, first=0, **how)
        tables = table_part(places, tall, **how)
        every = lax.all_gather(v, "outer")
        update, rest = decode_part(pod[None], every, *tables, x, wide, same, side)
        return rest[None, :, :width], update[:, :width]

    count = width // span
    each = count // chunks
    piece_cols = width // chunks
    ring = ring_order(members)
    position = jnp.where(me % 2 == 0, me // 2, members - 1 - me // 2)

    def ahead(d, steps):
        move = steps if d == 0 else -steps
        return [(ring[i], ring[(i + move) % members]) for i in range(members)]

    def owner(d, s):
        q = position - 1 - s + members if d == 0 else position + 1 + s
        return ring_at(lax.rem(q, members), members)

    def piece(source, d, s, j):
        start = owner(d, s) * width + j * piece_cols
        return lax.dynamic_slice(source, (d * side, start), (side, piece_cols))

    def tie(*arrays):
        return lax.optimization_barrier(arrays)

    def spans(a, j):
        return a[..., j * each : (j + 1) * each, :]

    last = members - 2
    cut = last - 1

    current = [[None] * 2 for _ in range(chunks)]
    token = ()
    for j in range(chunks):
        for d in range(2):
            source, *_ = tie(grad, *token)
            current[j][d] = piece(source, d, 0, j).astype(f32)
            token = (current[j][d],)

    def after(array):
        return tie(array, *token)[0]

    def terms(s, j):
        source = after(grad)
        return [piece(source, d, s, j) for d in range(2)]

    def own_filler(j):
        own[j] = own_part(
            mom,
            terms(members - 1, j),
            after(spans(own_places, j)),
            wide_t,
            tall,
            members=members,
            first=j * piece_cols,
            **how,
        )
        return own[j]

    def near_filler(j):
        raw[j] = term_part(terms(last, j), after(spans(near, j)), wide_t, tall, members=members, **how)
        return (raw[j],)

    def table_filler(j):
        tables[j] = table_part(after(spans(places, j)), tall, **how)
        return tables[j]

    def far_filler(j):
        sent[j] = term_part(current[j], after(spans(far, j)), wide_t, tall, members=members, **how)
        return (sent[j],)

    def moved(both, steps):
        parts = []
        for d in range(2):
            parts.append(lax.ppermute(both[d], "dev", ahead(d, steps)))
        return jnp.stack(parts)

    own, raw, tables, sent = ([None] * chunks for _ in range(4))
    arrivals = [[None] * 2 for _ in range(chunks)]
    fillers = {
        (0, 1): (own_filler, 0),
        (1, 0): (own_filler, 1),
        (1, 1): (near_filler, 0),
        (2, 0): (near_filler, 1),
        (2, 1): (table_filler, 0),
        (3, 0): (table_filler, 1),
        (cut - 1, 0): (far_filler, 0),
        (cut - 1, 1): (far_filler, 1),
    }
    for s in range(members - 1):
        for j in range(chunks):
            for d in range(2):
                arrived = lax.ppermute(current[j][d], "dev", ahead(d, 1))
                if s < last:
                    arrived, source, *_ = tie(arrived, grad, *token)
                    current[j][d] = arrived + piece(source, d, s + 1, j).astype(f32)
                    token = (current[j][d],)
                else:
                    arrivals[j][d] = arrived
            if (s, j) == (0, 0):
                places = after(chosen).reshape(pods, blocks, count, LANES)
                own_places = lax.dynamic_index_in_dim(places, pod, 0, keepdims=False)
                near = moved(own_places, -1)
                far = moved(own_places, -2)
            if (s, j) in fillers:
                fill, i = fillers[s, j]
                token += tuple(fill(i))
            if (s, j) == (2, 0):
                from_near = moved(jnp.concatenate(raw, axis=1), 1)
            if (s, j) == (cut - 1, 1):
                from_far = moved(jnp.concatenate(sent, axis=1), 2)
            if (s, j) == (cut, 1):
                values = jnp.concatenate([v for _, v in own], axis=1) + from_near + from_far
                every = lax.all_gather(after(values), "outer")
                token += (every,)
    updates, outs = [], []
    for j in range(chunks):
        update, rest = decode_part(pod[None], after(spans(every, j)), *tables[j], own[j][0], wide, same, side)
        token = (update,)
        updates.append(update)
        outs.append(rest + jnp.concatenate(arrivals[j], axis=0) / members)
    return jnp.concatenate(outs, axis=1)[None], jnp.concatenate(updates, axis=1)


def solution(mesh):
    def step(*args):
        return local(*args, pods=mesh.shape["outer"], members=mesh.shape["dev"])

    return jax.shard_map(
        step,
        mesh=mesh,
        in_specs=(
            P("outer", "dev", None, None),
            P("outer", None, "dev"),
            P(None, None, "dev", None),
        ),
        out_specs=(P("outer", None, "dev"), P(None, "dev")),
        check_vma=False,
    )
```

```python
import functools

import jax
import jax.numpy as jnp
import numpy as np
from jax import lax
from jax.experimental import pallas as pl
from jax.experimental.pallas import tpu as pltpu
from jax.sharding import PartitionSpec as P


GROUP = 64
LANES = 128

decay_rate = 0.999
tiny_eps = 1e-06


VMEM_LIMIT = 16 << 20
bf16 = jnp.bfloat16
f32 = jnp.float32


def cosine_basis(size):
    freq = np.arange(size, dtype=np.float64)[:, None]
    place = np.arange(size, dtype=np.float64)[None, :]
    weight = np.where(freq == 0, np.sqrt(1.0 / size), np.sqrt(2.0 / size))
    return (weight * np.cos(np.pi * (2.0 * place + 1.0) * freq / (2.0 * size))).astype(np.float32)


def halves_of(table):
    high = table.astype(bf16)
    return np.stack([high, (table - high.astype(np.float32)).astype(bf16)])


def split(x):
    high = x.astype(bf16)
    return high, (x - high.astype(f32)).astype(bf16)


def mm(a, b):
    return jnp.dot(a, b, preferred_element_type=f32)


def mm3(x, table):
    high, low = split(x)
    return mm(high, table[0]) + (mm(low, table[0]) + mm(high, table[1]))


def log2(n):
    assert n & (n - 1) == 0
    return n.bit_length() - 1


def table_places(idx, kept, side):
    lane = lax.broadcasted_iota(jnp.int32, idx.shape, 1)
    cell = (lane & (LANES - 1)) >> log2(kept)
    return idx >> log2(side), (cell << log2(side)) + (idx & (side - 1))


def one_hot(hit):
    return jnp.where(hit, 1.0, 0.0).astype(bf16)


def basis_rows(row, tall, side):
    at_row = one_hot(lax.broadcasted_iota(jnp.int32, (side, row.shape[1]), 0) == row)
    return mm(tall[0], at_row) + mm(tall[1], at_row)


def picks_of(xs, places, wide_t, tall, kept, side):
    high, low = split(mm3(jnp.concatenate(xs, axis=0), wide_t))
    found = []
    for i, idx in enumerate(places):
        row, col = table_places(idx, kept, side)
        at_col = one_hot(lax.broadcasted_iota(jnp.int32, (high.shape[1], idx.shape[1]), 0) == col)
        at = slice(i * side, (i + 1) * side)
        cols = mm(high[at], at_col) + mm(low[at], at_col)
        found.append(jnp.sum(cols * basis_rows(row, tall, side), axis=0, keepdims=True))
    return found


def in_hbm(a):
    return pltpu.with_memory_space_constraint(a, pltpu.HBM)


def in_vmem(a):
    return pltpu.with_memory_space_constraint(a, pltpu.VMEM)


ON_CHIP = pl.BlockSpec(memory_space=pltpu.VMEM)
PARAMS = pltpu.CompilerParams(vmem_limit_bytes=VMEM_LIMIT)


def cost(flops, moved):
    return pl.CostEstimate(flops=flops, bytes_accessed=moved, transcendentals=0)


def own_kernel(kept, side, members, first, mom_ref, *refs):
    *grad_refs, idx_ref, wide_t_ref, tall_ref, x_ref, v_ref = refs
    parts, count = idx_ref.shape[:2]
    span = wide_t_ref.shape[1]
    spots = [(r, q) for r in range(parts) for q in range(count)]
    xs = []
    for r, q in spots:
        rows = pl.ds(r * side, side)
        x = decay_rate * mom_ref[rows, pl.ds(first + q * span, span)]
        x += grad_refs[r][:, pl.ds(q * span, span)].astype(f32) / members
        x_ref[rows, pl.ds(q * span, span)] = x
        xs.append(x)
    places = [idx_ref[r, pl.ds(q, 1), :] for r, q in spots]
    for (r, q), v in zip(spots, picks_of(xs, places, wide_t_ref, tall_ref, kept, side)):
        v_ref[r, pl.ds(q, 1), :] = v


def own_part(mom, terms, idx, wide_t, tall, kept, side, members, first):
    shape = (mom.shape[0], terms[0].shape[1])
    size = shape[0] * shape[1]
    return pl.pallas_call(
        functools.partial(own_kernel, kept, side, members, first),
        out_shape=(pltpu.VMEM(shape, f32), jax.ShapeDtypeStruct(idx.shape, f32)),
        in_specs=[ON_CHIP] * (len(terms) + 4),
        out_specs=(ON_CHIP, ON_CHIP),
        compiler_params=PARAMS,
        cost_estimate=cost(size * wide_t.shape[1] * 10, size * 10),
    )(in_vmem(mom), *[in_vmem(x) for x in terms], idx, wide_t, tall)


def term_kernel(kept, side, members, *refs):
    *x_refs, idx_ref, wide_t_ref, tall_ref, v_ref = refs
    parts, count = idx_ref.shape[:2]
    span = wide_t_ref.shape[1]
    spots = [(r, q) for r in range(parts) for q in range(count)]
    xs = [x_refs[r][:, pl.ds(q * span, span)].astype(f32) for r, q in spots]
    places = [idx_ref[r, pl.ds(q, 1), :] for r, q in spots]
    for (r, q), v in zip(spots, picks_of(xs, places, wide_t_ref, tall_ref, kept, side)):
        v_ref[r, pl.ds(q, 1), :] = v / members


def term_part(terms, idx, wide_t, tall, kept, side, members):
    return pl.pallas_call(
        functools.partial(term_kernel, kept, side, members),
        out_shape=jax.ShapeDtypeStruct(idx.shape, f32),
        in_specs=[ON_CHIP] * (len(terms) + 3),
        out_specs=ON_CHIP,
        compiler_params=PARAMS,
        cost_estimate=cost(idx.size * side * wide_t.shape[1] * 40, idx.size * side * 4),
    )(*[in_vmem(x) for x in terms], idx, wide_t, tall)


def table_kernel(kept, side, idx_ref, tall_ref, rows_ref, cols_ref):
    pods, parts, count = idx_ref.shape[:3]
    span = cols_ref.shape[3]
    for r in range(parts):
        for q in range(count):
            idx = jnp.concatenate([idx_ref[p, r, pl.ds(q, 1), :] for p in range(pods)], axis=1)
            row, col = table_places(idx, kept, side)
            rows_ref[r, q] = basis_rows(row, tall_ref, side)
            tall_col = jnp.transpose(jnp.broadcast_to(col, (LANES, col.shape[1])))
            for c in range(0, span, LANES):
                lane = lax.broadcasted_iota(jnp.int32, tall_col.shape, 1) + c
                cols_ref[r, q, :, pl.ds(c, LANES)] = one_hot(tall_col == lane)


def table_part(idx, tall, kept, side):
    pods, parts, count, lanes = idx.shape
    span = LANES // kept * side
    return pl.pallas_call(
        functools.partial(table_kernel, kept, side),
        out_shape=(
            pltpu.VMEM((parts, count, side, pods * lanes), f32),
            pltpu.VMEM((parts, count, pods * lanes, span), bf16),
        ),
        in_specs=[ON_CHIP] * 2,
        out_specs=(ON_CHIP, ON_CHIP),
        compiler_params=PARAMS,
        cost_estimate=cost(parts * count * side * side * pods * lanes * 4, parts * count * pods * lanes * span * 2),
    )(idx, tall)


def decode_kernel(side, chunk, pod_ref, v_ref, rows_ref, cols_ref, x_ref, wide_ref, same_ref, *refs):
    update_hbm, rest_ref, table_ref, update_ref, sem_ref = refs[-5:]
    parts, count, _, lanes = rows_ref.shape
    pods, span = v_ref.shape[0], wide_ref.shape[1]
    mine = (lax.broadcasted_iota(jnp.int32, (1, lanes), 1) >> log2(LANES)) == pod_ref[0]
    for r in range(parts):
        for q in range(count):
            at = pl.ds(chunk * count + q, 1)
            v = jnp.concatenate([v_ref[p, r, at, :] for p in range(pods)], axis=1)
            rows = rows_ref[r, q]
            sides = jnp.concatenate([rows * v, rows * jnp.where(mine, v, 0.0)], axis=0)
            high, low = split(sides)
            table_ref[r * count + q] = mm(high, cols_ref[r, q]) + mm(low, cols_ref[r, q])
    table = table_ref[...].reshape(parts * count * 2 * side, span)
    spatial = mm3(table, wide_ref).reshape(parts * count, 2, side, span)
    shared = spatial[:, 0]
    squares = jnp.sum(shared * shared, axis=1) / (side * side)
    high, low = split(squares)
    mean = mm(high, same_ref[...]) + mm(low, same_ref[...])
    scale = 1.0 / jnp.sqrt(mean + tiny_eps)
    for r in range(parts):
        for q in range(count):
            at, b = (pl.ds(r * side, side), pl.ds(q * span, span)), r * count + q
            update_ref[at] = shared[b] * scale[b : b + 1, :]
    columns = pl.ds(chunk * update_ref.shape[1], update_ref.shape[1])
    copy = pltpu.make_async_copy(update_ref, update_hbm.at[:, columns], sem_ref)
    copy.start()
    for r in range(parts):
        for q in range(count):
            at, b = (pl.ds(r * side, side), pl.ds(q * span, span)), r * count + q
            rest_ref[at] = x_ref[at] - spatial[b, 1]
    copy.wait()


def decode_part(pod, values, tables, x, wide, same, side, chunk, chunks, update):
    rows, cols = tables
    parts, count = rows.shape[:2]
    height, width = x.shape
    held = [] if update is None else [update]
    hbm = pl.BlockSpec(memory_space=pl.ANY)
    return pl.pallas_call(
        functools.partial(decode_kernel, side, chunk),
        out_shape=(jax.ShapeDtypeStruct((height, chunks * width), f32), pltpu.VMEM(x.shape, f32)),
        in_specs=[pl.BlockSpec(memory_space=pltpu.SMEM)] + [ON_CHIP] * 6 + [hbm] * len(held),
        out_specs=(hbm, ON_CHIP),
        scratch_shapes=[
            pltpu.VMEM((parts * count, 2 * side, wide.shape[2]), f32),
            pltpu.VMEM(x.shape, f32),
            pltpu.SemaphoreType.DMA,
        ],
        input_output_aliases={7: 0} if held else {},
        compiler_params=PARAMS,
        cost_estimate=cost(x.size * wide.shape[2] * 20, x.size * 12),
    )(pod, values, in_vmem(rows), in_vmem(cols), in_vmem(x), wide, same, *held)


def finish_kernel(members, first, ways, rest_ref, *refs):
    arrived_refs, (out_ref, buffer_ref, sem_ref) = refs[:ways], refs[-3:]
    height, width = arrived_refs[0].shape
    copies = []
    for d, arrived_ref in enumerate(arrived_refs):
        rows = pl.ds(d * height, height)
        buffer_ref[rows, :] = rest_ref[rows, :] + arrived_ref[...] / members
        target = out_ref.at[rows, pl.ds(first, width)]
        copies.append(pltpu.make_async_copy(buffer_ref.at[rows], target, sem_ref.at[d]))
        copies[-1].start()
    for copy in copies:
        copy.wait()


def finish_part(out, columns, rest, arrived, members, first):
    held = [] if out is None else [out]
    hbm = pl.BlockSpec(memory_space=pl.ANY)
    return pl.pallas_call(
        functools.partial(finish_kernel, members, first, len(arrived)),
        out_shape=jax.ShapeDtypeStruct((rest.shape[0], columns), f32),
        in_specs=[ON_CHIP] * (1 + len(arrived)) + [hbm] * len(held),
        out_specs=hbm,
        scratch_shapes=[pltpu.VMEM(rest.shape, f32), pltpu.SemaphoreType.DMA((len(arrived),))],
        input_output_aliases={1 + len(arrived): 0} if held else {},
        compiler_params=PARAMS,
        cost_estimate=cost(rest.size, rest.size * 12),
    )(in_vmem(rest), *[in_vmem(a) for a in arrived], *held)


def ring_position(members):
    me = lax.axis_index("dev")
    return jnp.where((me & 1) == 0, me >> 1, members - 1 - (me >> 1))


def ring_owner(position, d, s, members):
    q = position - 1 - s if d == 0 else position + 1 + s
    q = jnp.where(q < 0, q + members, jnp.where(q >= members, q - members, q))
    return jnp.where(q < members // 2, 2 * q, 2 * members - 1 - 2 * q)


def load_kernel(members, side, j, s, ways, grad_ref, *refs):
    out_refs, (buffer_ref, sem_ref) = refs[-2 - len(ways) : -2], refs[-2:]
    arrived_refs = refs[: -2 - len(ways)]
    width = out_refs[0].shape[1]
    position = ring_position(members)
    chunks = grad_ref.shape[1] // (members * width)
    copies = []
    for i, d in enumerate(ways):
        start = pl.multiple_of((ring_owner(position, d, s, members) * chunks + j) * width, LANES)
        source = grad_ref.at[pl.ds(d * side, side), pl.ds(start, width)]
        copies.append(pltpu.make_async_copy(source, buffer_ref.at[i], sem_ref.at[i]))
        copies[-1].start()
    for i, copy in enumerate(copies):
        copy.wait()
        term = buffer_ref[i].astype(f32)
        out_refs[i][...] = arrived_refs[i][...] + term if arrived_refs else term


def load_part(grad, arrived, ways, j, s, members, side, width):
    return pl.pallas_call(
        functools.partial(load_kernel, members, side, j, s, ways),
        out_shape=[pltpu.VMEM((side, width), f32) for _ in ways],
        in_specs=[pl.BlockSpec(memory_space=pl.ANY)] + [ON_CHIP] * len(arrived),
        out_specs=[ON_CHIP] * len(ways),
        scratch_shapes=[pltpu.VMEM((len(ways), side, width), grad.dtype), pltpu.SemaphoreType.DMA((len(ways),))],
        compiler_params=PARAMS,
        cost_estimate=cost(side * width, side * width * 6),
    )(grad, *[in_vmem(a) for a in arrived])


def ring_order(n):
    return [2 * q if q < n // 2 else 2 * n - 1 - 2 * q for q in range(n)]


CHUNKS = 2
HOPS = 3
LEAST_RING = HOPS + 5


def local(gradients, momentum, chosen, pods, members):
    kept = chosen.shape[3]
    side = GROUP
    per = LANES // kept
    span = per * side
    grad, mom = gradients[0, 0], momentum[0]
    rows, width = mom.shape
    blocks = rows // side
    pod = lax.axis_index("outer")

    basis = cosine_basis(side)
    many = np.kron(np.eye(per, dtype=np.float32), basis)
    wide, wide_t, tall = (jnp.asarray(halves_of(t)) for t in (many, many.T, basis.T))
    same = jnp.asarray(np.kron(np.eye(per), np.ones((side, side))).astype(bf16))
    how = dict(kept=kept, side=side)

    chunks = CHUNKS
    if blocks != 2 or members % 2 or members < LEAST_RING or width % (chunks * span):
        summed = lax.psum_scatter(grad.astype(f32), "dev", scatter_dimension=1, tiled=True)
        pad = -width % span
        mom, summed = (jnp.pad(a, ((0, 0), (0, pad))) for a in (mom, summed))
        places = jnp.pad(chosen, ((0, 0), (0, 0), (0, pad // side), (0, 0)))
        count = (width + pad) // span
        places = places.reshape(pods, blocks, count, LANES)
        own_places = lax.dynamic_index_in_dim(places, pod, 0, keepdims=False)
        terms = [summed[r * side : (r + 1) * side] for r in range(blocks)]
        x, v = own_part(mom, terms, own_places, wide_t, tall, members=members, first=0, **how)
        tables = table_part(places, tall, **how)
        every = lax.all_gather(v, "outer")
        update, rest = decode_part(pod[None], every, tables, x, wide, same, side, 0, 1, None)
        return rest[None, :, :width], update[:, :width]

    count = width // span
    each = count // chunks
    piece_cols = width // chunks
    ring = ring_order(members)
    position = ring_position(members)

    def ahead(d, steps):
        move = steps if d == 0 else -steps
        return [(ring[i], ring[(i + move) % members]) for i in range(members)]

    def piece(source, d, s, j):
        start = ring_owner(position, d, s, members) * width + j * piece_cols
        return lax.dynamic_slice(source, (d * side, start), (side, piece_cols))

    def load(source, arrived, ways, j, s):
        return load_part(source, arrived, ways, j, s, members, side, piece_cols)

    def tie(*arrays):
        return lax.optimization_barrier(arrays)

    def spans(a, j):
        return a[..., j * each : (j + 1) * each, :]

    last = members - 2
    send = last + 1 - HOPS

    current = [[None] * 2 for _ in range(chunks)]
    token = ()
    for j in range(chunks):
        current[j] = list(load(tie(in_hbm(grad), *token)[0], (), (0, 1), j, 0))
        token = tuple(current[j])

    def after(array):
        return tie(array, *token)[0]

    def moved(both, steps):
        parts = []
        for d in range(2):
            parts.append(lax.ppermute(both[d], "dev", ahead(d, steps)))
        return jnp.stack(parts)

    places = after(chosen).reshape(pods, blocks, count, LANES)
    own_places = lax.dynamic_index_in_dim(places, pod, 0, keepdims=False)
    near = [moved(own_places, -steps) for steps in range(1, HOPS + 1)]

    def terms(s, j):
        source = after(grad)
        return [piece(source, d, s, j) for d in range(2)]

    def own_filler(j):
        own[j] = own_part(
            mom,
            terms(members - 1, j),
            after(spans(own_places, j)),
            wide_t,
            tall,
            members=members,
            first=j * piece_cols,
            **how,
        )
        return own[j]

    def raw_filler(j):
        others = [t for steps in range(1, HOPS) for t in terms(members - 1 - steps, j)]
        where = jnp.concatenate([spans(p, j) for p in near[: HOPS - 1]], axis=0)
        raw[j] = term_part(others, after(where), wide_t, tall, members=members, **how)
        return (raw[j],)

    def sent_filler(j):
        sent[j] = term_part(current[j], after(spans(near[-1], j)), wide_t, tall, members=members, **how)
        return (sent[j],)

    def table_filler(j):
        tables[j] = table_part(after(spans(places, j)), tall, **how)
        return tables[j]

    own, raw, tables, sent = ([None] * chunks for _ in range(4))
    arrivals = [[None] * 2 for _ in range(chunks)]
    fillers = {send - 3: raw_filler, send - 2: own_filler, send - 1: sent_filler, send: table_filler}
    for s in range(members - 1):
        for j in range(chunks):
            for d in range(2):
                arrived = lax.ppermute(current[j][d], "dev", ahead(d, 1))
                if s < last:
                    arrived, source, *_ = tie(arrived, grad, *token)
                    if s == 0:
                        (current[j][d],) = load(in_hbm(source), (arrived,), (d,), j, s + 1)
                    else:
                        current[j][d] = arrived + piece(source, d, s + 1, j).astype(f32)
                    token = (current[j][d],)
                else:
                    arrivals[j][d] = arrived
            if s in fillers:
                token += tuple(fillers[s](j))
            if (s, j) == (send - 3, chunks - 1):
                both = jnp.concatenate(raw, axis=1)
                received = [moved(both[2 * n - 2 : 2 * n], n) for n in range(1, HOPS)]
            if (s, j) == (send - 1, chunks - 1):
                received.append(moved(jnp.concatenate(sent, axis=1), HOPS))
            if (s, j) == (send + 1, 0):
                values = jnp.concatenate([v for _, v in own], axis=1) + sum(received)
                every = lax.all_gather(after(values), "outer")
                token += (every,)
    update, rests = None, []
    for j in range(chunks):
        update, rest = decode_part(pod[None], after(every), tables[j], own[j][0], wide, same, side, j, chunks, update)
        rests.append(rest)
    out = None
    for j in range(chunks):
        out = finish_part(out, width, rests[j], arrivals[j], members, j * piece_cols)
    return out[None], update


def solution(mesh):
    def step(*args):
        return local(*args, pods=mesh.shape["outer"], members=mesh.shape["dev"])

    return jax.shard_map(
        step,
        mesh=mesh,
        in_specs=(
            P("outer", "dev", None, None),
            P("outer", None, "dev"),
            P(None, None, "dev", None),
        ),
        out_specs=(P("outer", None, "dev"), P(None, "dev")),
        check_vma=False,
    )
```

```python
import functools

import jax
import jax.numpy as jnp
import numpy as np
from jax import lax
from jax.experimental import pallas as pl
from jax.experimental.pallas import tpu as pltpu
from jax.sharding import PartitionSpec as P


GROUP = 64
LANES = 128

decay_rate = 0.999
tiny_eps = 1e-06


VMEM_LIMIT = 16 << 20
bf16 = jnp.bfloat16
f32 = jnp.float32


def cosine_basis(size):
    freq = np.arange(size, dtype=np.float64)[:, None]
    place = np.arange(size, dtype=np.float64)[None, :]
    weight = np.where(freq == 0, np.sqrt(1.0 / size), np.sqrt(2.0 / size))
    return (weight * np.cos(np.pi * (2.0 * place + 1.0) * freq / (2.0 * size))).astype(np.float32)


def parts_of(table):
    parts = []
    for _ in range(3):
        parts.append(table.astype(bf16))
        table = table - parts[-1].astype(np.float32)
    return np.stack(parts)


def split(x, count=3):
    parts = []
    for _ in range(count):
        parts.append(x.astype(bf16))
        x = x - parts[-1].astype(f32)
    return parts


def mm(a, b):
    return jnp.dot(a, b, preferred_element_type=f32)


def pick(x, one_hots, count=3):
    return sum(mm(part, one_hots) for part in reversed(split(x, count)))


def product(x, table):
    if x.dtype == bf16:
        return mm(x, table[0]) + (mm(x, table[1]) + mm(x, table[2]))
    high, middle, low = split(x)
    small = mm(low, table[0]) + (mm(middle, table[1]) + mm(high, table[2]))
    return mm(high, table[0]) + (mm(middle, table[0]) + (mm(high, table[1]) + small))


def log2(n):
    assert n & (n - 1) == 0
    return n.bit_length() - 1


def table_places(idx, kept, side):
    lane = lax.broadcasted_iota(jnp.int32, idx.shape, 1)
    cell = (lane & (LANES - 1)) >> log2(kept)
    return idx >> log2(side), (cell << log2(side)) + (idx & (side - 1))


def one_hot(hit):
    return jnp.where(hit, 1.0, 0.0).astype(bf16)


def basis_rows(row, tall, side):
    at_row = one_hot(lax.broadcasted_iota(jnp.int32, (side, row.shape[1]), 0) == row)
    return mm(tall[0], at_row) + (mm(tall[1], at_row) + mm(tall[2], at_row))


def picks_of(xs, places, wide_t, tall, kept, side):
    spectra = product(jnp.concatenate(xs, axis=0), wide_t)
    found = []
    for i, idx in enumerate(places):
        row, col = table_places(idx, kept, side)
        at_col = one_hot(lax.broadcasted_iota(jnp.int32, (spectra.shape[1], idx.shape[1]), 0) == col)
        cols = pick(spectra[i * side : (i + 1) * side], at_col)
        found.append(jnp.sum(cols * basis_rows(row, tall, side), axis=0, keepdims=True))
    return found


def in_hbm(a):
    return pltpu.with_memory_space_constraint(a, pltpu.HBM)


def in_vmem(a):
    return pltpu.with_memory_space_constraint(a, pltpu.VMEM)


ON_CHIP = pl.BlockSpec(memory_space=pltpu.VMEM)
PARAMS = pltpu.CompilerParams(vmem_limit_bytes=VMEM_LIMIT)


def cost(flops, moved):
    return pl.CostEstimate(flops=flops, bytes_accessed=moved, transcendentals=0)


def own_kernel(kept, side, members, first, mom_ref, *refs):
    *grad_refs, idx_ref, wide_t_ref, tall_ref, x_ref, v_ref = refs
    parts, count = idx_ref.shape[:2]
    span = wide_t_ref.shape[1]
    spots = [(r, q) for r in range(parts) for q in range(count)]
    xs = []
    for r, q in spots:
        rows = pl.ds(r * side, side)
        x = decay_rate * mom_ref[rows, pl.ds(first + q * span, span)]
        x += grad_refs[r][:, pl.ds(q * span, span)].astype(f32) / members
        x_ref[rows, pl.ds(q * span, span)] = x
        xs.append(x)
    places = [idx_ref[r, q] for r, q in spots]
    for (r, q), v in zip(spots, picks_of(xs, places, wide_t_ref, tall_ref, kept, side)):
        v_ref[r, q] = v


def own_part(mom, terms, idx, wide_t, tall, kept, side, members, first):
    shape = (mom.shape[0], terms[0].shape[1])
    size = shape[0] * shape[1]
    return pl.pallas_call(
        functools.partial(own_kernel, kept, side, members, first),
        out_shape=(pltpu.VMEM(shape, f32), jax.ShapeDtypeStruct(idx.shape, f32)),
        in_specs=[ON_CHIP] * (len(terms) + 4),
        out_specs=(ON_CHIP, ON_CHIP),
        compiler_params=PARAMS,
        cost_estimate=cost(size * wide_t.shape[1] * 10, size * 10),
    )(in_vmem(mom), *[in_vmem(x) for x in terms], idx, wide_t, tall)


def term_kernel(kept, side, members, *refs):
    *x_refs, idx_ref, wide_t_ref, tall_ref, v_ref = refs
    parts, count = idx_ref.shape[:2]
    span = wide_t_ref.shape[1]
    spots = [(r, q) for r in range(parts) for q in range(count)]
    xs = [x_refs[r][:, pl.ds(q * span, span)] for r, q in spots]
    places = [idx_ref[r, q] for r, q in spots]
    for (r, q), v in zip(spots, picks_of(xs, places, wide_t_ref, tall_ref, kept, side)):
        v_ref[r, q] = v / members


def term_part(terms, idx, wide_t, tall, kept, side, members):
    return pl.pallas_call(
        functools.partial(term_kernel, kept, side, members),
        out_shape=jax.ShapeDtypeStruct(idx.shape, f32),
        in_specs=[ON_CHIP] * (len(terms) + 3),
        out_specs=ON_CHIP,
        compiler_params=PARAMS,
        cost_estimate=cost(idx.size * side * wide_t.shape[1] * 40, idx.size * side * 4),
    )(*[in_vmem(x) for x in terms], idx, wide_t, tall)


def table_kernel(kept, side, idx_ref, tall_ref, rows_ref, cols_ref):
    pods, parts, count = idx_ref.shape[:3]
    span = cols_ref.shape[3]
    for r in range(parts):
        for q in range(count):
            idx = jnp.concatenate([idx_ref[p, r, q] for p in range(pods)], axis=1)
            row, col = table_places(idx, kept, side)
            rows_ref[r, q] = basis_rows(row, tall_ref, side)
            tall_col = jnp.transpose(jnp.broadcast_to(col, (LANES, col.shape[1])))
            for c in range(0, span, LANES):
                lane = lax.broadcasted_iota(jnp.int32, tall_col.shape, 1) + c
                cols_ref[r, q, :, pl.ds(c, LANES)] = one_hot(tall_col == lane)


def table_part(idx, tall, kept, side):
    pods, parts, count, _, lanes = idx.shape
    span = LANES // kept * side
    return pl.pallas_call(
        functools.partial(table_kernel, kept, side),
        out_shape=(
            pltpu.VMEM((parts, count, side, pods * lanes), f32),
            pltpu.VMEM((parts, count, pods * lanes, span), bf16),
        ),
        in_specs=[ON_CHIP] * 2,
        out_specs=(ON_CHIP, ON_CHIP),
        compiler_params=PARAMS,
        cost_estimate=cost(parts * count * side * side * pods * lanes * 4, parts * count * pods * lanes * span * 2),
    )(idx, tall)


def decode_kernel(side, chunk, pod_ref, v_ref, rows_ref, cols_ref, x_ref, wide_ref, same_ref, *refs):
    update_hbm, rest_ref, table_ref, update_ref, sem_ref = refs[-5:]
    parts, count, _, lanes = rows_ref.shape
    pods, span = v_ref.shape[0], wide_ref.shape[1]
    mine = (lax.broadcasted_iota(jnp.int32, (1, lanes), 1) >> log2(LANES)) == pod_ref[0]
    for r in range(parts):
        for q in range(count):
            v = jnp.concatenate([v_ref[p, r, chunk * count + q] for p in range(pods)], axis=1)
            rows = rows_ref[r, q]
            sides = jnp.concatenate([rows * v, rows * jnp.where(mine, v, 0.0)], axis=0)
            table_ref[r * count + q] = pick(sides, cols_ref[r, q])
    table = table_ref[...].reshape(parts * count * 2 * side, span)
    spatial = product(table, wide_ref).reshape(parts * count, 2, side, span)
    shared = spatial[:, 0]
    squares = jnp.sum(shared * shared, axis=1) / (side * side)
    mean = pick(squares, same_ref[...])
    scale = 1.0 / jnp.sqrt(mean + tiny_eps)
    for r in range(parts):
        for q in range(count):
            at, b = (pl.ds(r * side, side), pl.ds(q * span, span)), r * count + q
            update_ref[at] = shared[b] * scale[b : b + 1, :]
    columns = pl.ds(chunk * update_ref.shape[1], update_ref.shape[1])
    copy = pltpu.make_async_copy(update_ref, update_hbm.at[:, columns], sem_ref)
    copy.start()
    for r in range(parts):
        for q in range(count):
            at, b = (pl.ds(r * side, side), pl.ds(q * span, span)), r * count + q
            rest_ref[at] = x_ref[at] - spatial[b, 1]
    copy.wait()


def decode_part(pod, values, tables, x, wide, same, side, chunk, chunks, update):
    rows, cols = tables
    parts, count = rows.shape[:2]
    height, width = x.shape
    held = [] if update is None else [update]
    hbm = pl.BlockSpec(memory_space=pl.ANY)
    return pl.pallas_call(
        functools.partial(decode_kernel, side, chunk),
        out_shape=(jax.ShapeDtypeStruct((height, chunks * width), f32), pltpu.VMEM(x.shape, f32)),
        in_specs=[pl.BlockSpec(memory_space=pltpu.SMEM)] + [ON_CHIP] * 6 + [hbm] * len(held),
        out_specs=(hbm, ON_CHIP),
        scratch_shapes=[
            pltpu.VMEM((parts * count, 2 * side, wide.shape[2]), f32),
            pltpu.VMEM(x.shape, f32),
            pltpu.SemaphoreType.DMA,
        ],
        input_output_aliases={7: 0} if held else {},
        compiler_params=PARAMS,
        cost_estimate=cost(x.size * wide.shape[2] * 20, x.size * 12),
    )(pod, values, in_vmem(rows), in_vmem(cols), in_vmem(x), wide, same, *held)


def finish_kernel(members, first, ways, rest_ref, *refs):
    arrived_refs, (out_ref, buffer_ref, sem_ref) = refs[:ways], refs[-3:]
    height, width = arrived_refs[0].shape
    copies = []
    for d, arrived_ref in enumerate(arrived_refs):
        rows = pl.ds(d * height, height)
        buffer_ref[rows, :] = rest_ref[rows, :] + arrived_ref[...] / members
        target = out_ref.at[rows, pl.ds(first, width)]
        copies.append(pltpu.make_async_copy(buffer_ref.at[rows], target, sem_ref.at[d]))
        copies[-1].start()
    for copy in copies:
        copy.wait()


def finish_part(out, columns, rest, arrived, members, first):
    held = [] if out is None else [out]
    hbm = pl.BlockSpec(memory_space=pl.ANY)
    return pl.pallas_call(
        functools.partial(finish_kernel, members, first, len(arrived)),
        out_shape=jax.ShapeDtypeStruct((rest.shape[0], columns), f32),
        in_specs=[ON_CHIP] * (1 + len(arrived)) + [hbm] * len(held),
        out_specs=hbm,
        scratch_shapes=[pltpu.VMEM(rest.shape, f32), pltpu.SemaphoreType.DMA((len(arrived),))],
        input_output_aliases={1 + len(arrived): 0} if held else {},
        compiler_params=PARAMS,
        cost_estimate=cost(rest.size, rest.size * 12),
    )(in_vmem(rest), *[in_vmem(a) for a in arrived], *held)


def ring_position(members):
    me = lax.axis_index("dev")
    return jnp.where((me & 1) == 0, me >> 1, members - 1 - (me >> 1))


def ring_owner(position, d, s, members):
    q = position - 1 - s if d == 0 else position + 1 + s
    q = jnp.where(q < 0, q + members, jnp.where(q >= members, q - members, q))
    return jnp.where(q < members // 2, 2 * q, 2 * members - 1 - 2 * q)


def load_kernel(members, side, j, s, ways, grad_ref, *refs):
    out_refs, (buffer_ref, sem_ref) = refs[-2 - len(ways) : -2], refs[-2:]
    arrived_refs = refs[: -2 - len(ways)]
    width = out_refs[0].shape[1]
    position = ring_position(members)
    chunks = grad_ref.shape[1] // (members * width)
    copies = []
    for i, d in enumerate(ways):
        start = pl.multiple_of((ring_owner(position, d, s, members) * chunks + j) * width, LANES)
        source = grad_ref.at[pl.ds(d * side, side), pl.ds(start, width)]
        copies.append(pltpu.make_async_copy(source, buffer_ref.at[i], sem_ref.at[i]))
        copies[-1].start()
    for i, copy in enumerate(copies):
        copy.wait()
        term = buffer_ref[i].astype(f32)
        out_refs[i][...] = arrived_refs[i][...] + term if arrived_refs else term


def load_part(grad, arrived, ways, j, s, members, side, width):
    return pl.pallas_call(
        functools.partial(load_kernel, members, side, j, s, ways),
        out_shape=[pltpu.VMEM((side, width), f32) for _ in ways],
        in_specs=[pl.BlockSpec(memory_space=pl.ANY)] + [ON_CHIP] * len(arrived),
        out_specs=[ON_CHIP] * len(ways),
        scratch_shapes=[pltpu.VMEM((len(ways), side, width), grad.dtype), pltpu.SemaphoreType.DMA((len(ways),))],
        compiler_params=PARAMS,
        cost_estimate=cost(side * width, side * width * 6),
    )(grad, *[in_vmem(a) for a in arrived])


def ring_order(n):
    return [2 * q if q < n // 2 else 2 * n - 1 - 2 * q for q in range(n)]


CHUNKS = 2
HOPS = 3
LEAST_RING = HOPS + 5


def local(gradients, momentum, chosen, pods, members):
    kept = chosen.shape[3]
    side = GROUP
    per = LANES // kept
    span = per * side
    grad, mom = gradients[0, 0], momentum[0]
    rows, width = mom.shape
    blocks = rows // side
    pod = lax.axis_index("outer")

    basis = cosine_basis(side)
    many = np.kron(np.eye(per, dtype=np.float32), basis)
    wide, wide_t, tall = (jnp.asarray(parts_of(t)) for t in (many, many.T, basis.T))
    same = jnp.asarray(np.kron(np.eye(per), np.ones((side, side))).astype(bf16))
    how = dict(kept=kept, side=side)

    chunks = CHUNKS
    if blocks != 2 or members % 2 or members < LEAST_RING or width % (chunks * span):
        summed = lax.psum_scatter(grad.astype(f32), "dev", scatter_dimension=1, tiled=True)
        pad = -width % span
        mom, summed = (jnp.pad(a, ((0, 0), (0, pad))) for a in (mom, summed))
        places = jnp.pad(chosen, ((0, 0), (0, 0), (0, pad // side), (0, 0)))
        count = (width + pad) // span
        places = places.reshape(pods, blocks, count, 1, LANES)
        own_places = lax.dynamic_index_in_dim(places, pod, 0, keepdims=False)
        terms = [summed[r * side : (r + 1) * side] for r in range(blocks)]
        x, v = own_part(mom, terms, own_places, wide_t, tall, members=members, first=0, **how)
        tables = table_part(places, tall, **how)
        every = lax.all_gather(v, "outer")
        update, rest = decode_part(pod[None], every, tables, x, wide, same, side, 0, 1, None)
        return rest[None, :, :width], update[:, :width]

    count = width // span
    each = count // chunks
    piece_cols = width // chunks
    ring = ring_order(members)
    position = ring_position(members)

    def ahead(d, steps):
        move = steps if d == 0 else -steps
        return [(ring[i], ring[(i + move) % members]) for i in range(members)]

    def piece(source, d, s, j):
        start = ring_owner(position, d, s, members) * width + j * piece_cols
        return lax.dynamic_slice(source, (d * side, start), (side, piece_cols))

    def load(source, arrived, ways, j, s):
        return load_part(source, arrived, ways, j, s, members, side, piece_cols)

    def tie(*arrays):
        return lax.optimization_barrier(arrays)

    def spans(a, j):
        return a[..., j * each : (j + 1) * each, :, :]

    last = members - 2
    send = last + 1 - HOPS

    current = [[None] * 2 for _ in range(chunks)]
    token = ()
    for j in range(chunks):
        current[j] = list(load(tie(in_hbm(grad), *token)[0], (), (0, 1), j, 0))
        token = tuple(current[j])

    def after(array):
        return tie(array, *token)[0]

    def moved(both, steps):
        parts = []
        for d in range(2):
            parts.append(lax.ppermute(both[d], "dev", ahead(d, steps)))
        return jnp.stack(parts)

    places = after(chosen).reshape(pods, blocks, count, 1, LANES)
    own_places = lax.dynamic_index_in_dim(places, pod, 0, keepdims=False)
    near = [own_places]
    for _ in range(1, HOPS + 1):
        near.append(moved(near[-1], -1))
    near = near[1:]

    def terms(s, j):
        source = after(grad)
        return [piece(source, d, s, j) for d in range(2)]

    def own_filler(j):
        own[j] = own_part(
            mom,
            terms(members - 1, j),
            after(spans(own_places, j)),
            wide_t,
            tall,
            members=members,
            first=j * piece_cols,
            **how,
        )
        return own[j]

    def raw_filler(j):
        others = [t for steps in range(1, HOPS) for t in terms(members - 1 - steps, j)]
        where = jnp.concatenate([spans(p, j) for p in near[: HOPS - 1]], axis=0)
        raw[j] = term_part(others, after(where), wide_t, tall, members=members, **how)
        return (raw[j],)

    def sent_filler(j):
        sent[j] = term_part(current[j], after(spans(near[-1], j)), wide_t, tall, members=members, **how)
        return (sent[j],)

    def table_filler(j):
        tables[j] = table_part(after(spans(places, j)), tall, **how)
        return tables[j]

    own, raw, tables, sent = ([None] * chunks for _ in range(4))
    arrivals = [[None] * 2 for _ in range(chunks)]
    fillers = {send - 3: own_filler, send - 2: raw_filler, send - 1: sent_filler, send: table_filler}
    for s in range(members - 1):
        for j in range(chunks):
            for d in range(2):
                arrived = lax.ppermute(current[j][d], "dev", ahead(d, 1))
                if s < last:
                    arrived, source, *_ = tie(arrived, grad, *token)
                    if s == 0:
                        (current[j][d],) = load(in_hbm(source), (arrived,), (d,), j, s + 1)
                    else:
                        current[j][d] = arrived + piece(source, d, s + 1, j).astype(f32)
                    token = (current[j][d],)
                else:
                    arrivals[j][d] = arrived
            if s in fillers:
                token += tuple(fillers[s](j))
            if (s, j) == (send - 2, chunks - 1):
                both = jnp.concatenate(raw, axis=1)
                received = [moved(both[2 * n - 2 : 2 * n], n) for n in range(1, HOPS)]
            if (s, j) == (send - 1, chunks - 1):
                received.append(moved(jnp.concatenate(sent, axis=1), HOPS))
            if (s, j) == (send + 1, 0):
                values = jnp.concatenate([v for _, v in own], axis=1) + sum(received)
                every = lax.all_gather(after(values), "outer")
                token += (every,)
    update, rests = None, []
    for j in range(chunks):
        update, rest = decode_part(pod[None], after(every), tables[j], own[j][0], wide, same, side, j, chunks, update)
        rests.append(rest)
    out = None
    for j in range(chunks):
        out = finish_part(out, width, rests[j], arrivals[j], members, j * piece_cols)
    return out[None], update


def solution(mesh):
    def step(*args):
        return local(*args, pods=mesh.shape["outer"], members=mesh.shape["dev"])

    return jax.shard_map(
        step,
        mesh=mesh,
        in_specs=(
            P("outer", "dev", None, None),
            P("outer", None, "dev"),
            P(None, None, "dev", None),
        ),
        out_specs=(P("outer", None, "dev"), P(None, "dev")),
        check_vma=False,
    )
```

```python
import functools

import jax
import jax.numpy as jnp
import numpy as np
from jax import lax
from jax.experimental import pallas as pl
from jax.experimental.pallas import tpu as pltpu
from jax.sharding import PartitionSpec as P


GROUP = 64
LANES = 128

decay_rate = 0.999
tiny_eps = 1e-06


VMEM_LIMIT = 16 << 20
bf16 = jnp.bfloat16
f32 = jnp.float32


def cosine_basis(size):
    freq = np.arange(size, dtype=np.float64)[:, None]
    place = np.arange(size, dtype=np.float64)[None, :]
    weight = np.where(freq == 0, np.sqrt(1.0 / size), np.sqrt(2.0 / size))
    return (weight * np.cos(np.pi * (2.0 * place + 1.0) * freq / (2.0 * size))).astype(np.float32)


def parts_of(table):
    parts = []
    for _ in range(3):
        parts.append(table.astype(bf16))
        table = table - parts[-1].astype(np.float32)
    return np.stack(parts)


def split(x, count=3):
    parts = []
    for _ in range(count):
        parts.append(x.astype(bf16))
        x = x - parts[-1].astype(f32)
    return parts


def mm(a, b):
    return jnp.dot(a, b, preferred_element_type=f32)


def pick(x, one_hots, count=3):
    return sum(mm(part, one_hots) for part in reversed(split(x, count)))


def product(x, table):
    if x.dtype == bf16:
        return mm(x, table[0]) + (mm(x, table[1]) + mm(x, table[2]))
    high, middle, low = split(x)
    small = mm(low, table[0]) + (mm(middle, table[1]) + mm(high, table[2]))
    return mm(high, table[0]) + (mm(middle, table[0]) + (mm(high, table[1]) + small))


def log2(n):
    assert n & (n - 1) == 0
    return n.bit_length() - 1


def table_places(idx, kept, side):
    lane = lax.broadcasted_iota(jnp.int32, idx.shape, 1)
    cell = (lane & (LANES - 1)) >> log2(kept)
    return idx >> log2(side), (cell << log2(side)) + (idx & (side - 1))


def one_hot(hit):
    return jnp.where(hit, 1.0, 0.0).astype(bf16)


def basis_rows(row, tall, side):
    at_row = one_hot(lax.broadcasted_iota(jnp.int32, (side, row.shape[1]), 0) == row)
    return mm(tall[0], at_row) + (mm(tall[1], at_row) + mm(tall[2], at_row))


def picks_of(xs, places, wide_t, tall, kept, side):
    spectra = product(jnp.concatenate(xs, axis=0), wide_t)
    found = []
    for i, idx in enumerate(places):
        row, col = table_places(idx, kept, side)
        at_col = one_hot(lax.broadcasted_iota(jnp.int32, (spectra.shape[1], idx.shape[1]), 0) == col)
        cols = pick(spectra[i * side : (i + 1) * side], at_col)
        found.append(jnp.sum(cols * basis_rows(row, tall, side), axis=0, keepdims=True))
    return found


def in_hbm(a):
    return pltpu.with_memory_space_constraint(a, pltpu.HBM)


def in_vmem(a):
    return pltpu.with_memory_space_constraint(a, pltpu.VMEM)


ON_CHIP = pl.BlockSpec(memory_space=pltpu.VMEM)
PARAMS = pltpu.CompilerParams(vmem_limit_bytes=VMEM_LIMIT)


def cost(flops, moved):
    return pl.CostEstimate(flops=flops, bytes_accessed=moved, transcendentals=0)


def own_kernel(kept, side, members, first, mom_ref, *refs):
    *grad_refs, idx_ref, wide_t_ref, tall_ref, x_ref, v_ref = refs
    parts, count = idx_ref.shape[:2]
    span = wide_t_ref.shape[1]
    spots = [(r, q) for r in range(parts) for q in range(count)]
    xs = []
    for r, q in spots:
        rows = pl.ds(r * side, side)
        x = decay_rate * mom_ref[rows, pl.ds(first + q * span, span)]
        x += grad_refs[r][:, pl.ds(q * span, span)].astype(f32) / members
        x_ref[rows, pl.ds(q * span, span)] = x
        xs.append(x)
    places = [idx_ref[r, q] for r, q in spots]
    for (r, q), v in zip(spots, picks_of(xs, places, wide_t_ref, tall_ref, kept, side)):
        v_ref[r, q] = v


def own_part(mom, terms, idx, wide_t, tall, kept, side, members, first):
    shape = (mom.shape[0], terms[0].shape[1])
    size = shape[0] * shape[1]
    return pl.pallas_call(
        functools.partial(own_kernel, kept, side, members, first),
        out_shape=(pltpu.VMEM(shape, f32), jax.ShapeDtypeStruct(idx.shape, f32)),
        in_specs=[ON_CHIP] * (len(terms) + 4),
        out_specs=(ON_CHIP, ON_CHIP),
        compiler_params=PARAMS,
        cost_estimate=cost(size * wide_t.shape[1] * 10, size * 10),
    )(in_vmem(mom), *[in_vmem(x) for x in terms], idx, wide_t, tall)


def term_kernel(kept, side, members, *refs):
    *x_refs, idx_ref, wide_t_ref, tall_ref, v_ref = refs
    parts, count = idx_ref.shape[:2]
    span = wide_t_ref.shape[1]
    spots = [(r, q) for r in range(parts) for q in range(count)]
    xs = [x_refs[r][:, pl.ds(q * span, span)] for r, q in spots]
    places = [idx_ref[r, q] for r, q in spots]
    for (r, q), v in zip(spots, picks_of(xs, places, wide_t_ref, tall_ref, kept, side)):
        v_ref[r, q] = v / members


def term_part(terms, idx, wide_t, tall, kept, side, members):
    return pl.pallas_call(
        functools.partial(term_kernel, kept, side, members),
        out_shape=jax.ShapeDtypeStruct(idx.shape, f32),
        in_specs=[ON_CHIP] * (len(terms) + 3),
        out_specs=ON_CHIP,
        compiler_params=PARAMS,
        cost_estimate=cost(idx.size * side * wide_t.shape[1] * 40, idx.size * side * 4),
    )(*[in_vmem(x) for x in terms], idx, wide_t, tall)


def table_kernel(kept, side, idx_ref, tall_ref, rows_ref, cols_ref):
    pods, parts, count = idx_ref.shape[:3]
    span = cols_ref.shape[3]
    for r in range(parts):
        for q in range(count):
            idx = jnp.concatenate([idx_ref[p, r, q] for p in range(pods)], axis=1)
            row, col = table_places(idx, kept, side)
            rows_ref[r, q] = basis_rows(row, tall_ref, side)
            tall_col = jnp.transpose(jnp.broadcast_to(col, (LANES, col.shape[1])))
            for c in range(0, span, LANES):
                lane = lax.broadcasted_iota(jnp.int32, tall_col.shape, 1) + c
                cols_ref[r, q, :, pl.ds(c, LANES)] = one_hot(tall_col == lane)


def table_part(idx, tall, kept, side):
    pods, parts, count, _, lanes = idx.shape
    span = LANES // kept * side
    return pl.pallas_call(
        functools.partial(table_kernel, kept, side),
        out_shape=(
            pltpu.VMEM((parts, count, side, pods * lanes), f32),
            pltpu.VMEM((parts, count, pods * lanes, span), bf16),
        ),
        in_specs=[ON_CHIP] * 2,
        out_specs=(ON_CHIP, ON_CHIP),
        compiler_params=PARAMS,
        cost_estimate=cost(parts * count * side * side * pods * lanes * 4, parts * count * pods * lanes * span * 2),
    )(idx, tall)


def decode_kernel(side, chunk, pod_ref, v_ref, rows_ref, cols_ref, x_ref, wide_ref, same_ref, *refs):
    update_hbm, rest_ref, table_ref, update_ref, sem_ref = refs[-5:]
    parts, count, _, lanes = rows_ref.shape
    pods, span = v_ref.shape[0], wide_ref.shape[1]
    mine = (lax.broadcasted_iota(jnp.int32, (1, lanes), 1) >> log2(LANES)) == pod_ref[0]
    for r in range(parts):
        for q in range(count):
            v = jnp.concatenate([v_ref[p, r, chunk * count + q] for p in range(pods)], axis=1)
            rows = rows_ref[r, q]
            sides = jnp.concatenate([rows * v, rows * jnp.where(mine, v, 0.0)], axis=0)
            table_ref[r * count + q] = pick(sides, cols_ref[r, q])
    table = table_ref[...].reshape(parts * count * 2 * side, span)
    spatial = product(table, wide_ref).reshape(parts * count, 2, side, span)
    shared = spatial[:, 0]
    squares = jnp.sum(shared * shared, axis=1) / (side * side)
    mean = pick(squares, same_ref[...])
    scale = 1.0 / jnp.sqrt(mean + tiny_eps)
    for r in range(parts):
        for q in range(count):
            at, b = (pl.ds(r * side, side), pl.ds(q * span, span)), r * count + q
            update_ref[at] = shared[b] * scale[b : b + 1, :]
    columns = pl.ds(chunk * update_ref.shape[1], update_ref.shape[1])
    copy = pltpu.make_async_copy(update_ref, update_hbm.at[:, columns], sem_ref)
    copy.start()
    for r in range(parts):
        for q in range(count):
            at, b = (pl.ds(r * side, side), pl.ds(q * span, span)), r * count + q
            rest_ref[at] = x_ref[at] - spatial[b, 1]
    copy.wait()


def decode_part(pod, values, tables, x, wide, same, side, chunk, chunks, update):
    rows, cols = tables
    parts, count = rows.shape[:2]
    height, width = x.shape
    held = [] if update is None else [update]
    hbm = pl.BlockSpec(memory_space=pl.ANY)
    return pl.pallas_call(
        functools.partial(decode_kernel, side, chunk),
        out_shape=(jax.ShapeDtypeStruct((height, chunks * width), f32), pltpu.VMEM(x.shape, f32)),
        in_specs=[pl.BlockSpec(memory_space=pltpu.SMEM)] + [ON_CHIP] * 6 + [hbm] * len(held),
        out_specs=(hbm, ON_CHIP),
        scratch_shapes=[
            pltpu.VMEM((parts * count, 2 * side, wide.shape[2]), f32),
            pltpu.VMEM(x.shape, f32),
            pltpu.SemaphoreType.DMA,
        ],
        input_output_aliases={7: 0} if held else {},
        compiler_params=PARAMS,
        cost_estimate=cost(x.size * wide.shape[2] * 20, x.size * 12),
    )(pod, values, in_vmem(rows), in_vmem(cols), in_vmem(x), wide, same, *held)


def finish_kernel(members, first, ways, rest_ref, *refs):
    arrived_refs, (out_ref, buffer_ref, sem_ref) = refs[:ways], refs[-3:]
    height, width = arrived_refs[0].shape
    copies = []
    for d, arrived_ref in enumerate(arrived_refs):
        rows = pl.ds(d * height, height)
        buffer_ref[rows, :] = rest_ref[rows, :] + arrived_ref[...] / members
        target = out_ref.at[rows, pl.ds(first, width)]
        copies.append(pltpu.make_async_copy(buffer_ref.at[rows], target, sem_ref.at[d]))
        copies[-1].start()
    for copy in copies:
        copy.wait()


def finish_part(out, columns, rest, arrived, members, first):
    held = [] if out is None else [out]
    hbm = pl.BlockSpec(memory_space=pl.ANY)
    return pl.pallas_call(
        functools.partial(finish_kernel, members, first, len(arrived)),
        out_shape=jax.ShapeDtypeStruct((rest.shape[0], columns), f32),
        in_specs=[ON_CHIP] * (1 + len(arrived)) + [hbm] * len(held),
        out_specs=hbm,
        scratch_shapes=[pltpu.VMEM(rest.shape, f32), pltpu.SemaphoreType.DMA((len(arrived),))],
        input_output_aliases={1 + len(arrived): 0} if held else {},
        compiler_params=PARAMS,
        cost_estimate=cost(rest.size, rest.size * 12),
    )(in_vmem(rest), *[in_vmem(a) for a in arrived], *held)


def ring_position(members):
    me = lax.axis_index("dev")
    return jnp.where((me & 1) == 0, me >> 1, members - 1 - (me >> 1))


def ring_owner(position, d, s, members):
    q = position - 1 - s if d == 0 else position + 1 + s
    q = jnp.where(q < 0, q + members, jnp.where(q >= members, q - members, q))
    return jnp.where(q < members // 2, 2 * q, 2 * members - 1 - 2 * q)


def stage_kernel(members, side, j, s, ways, grad_ref, *refs):
    out_refs, sem_ref = refs[:-1], refs[-1]
    width = out_refs[0].shape[1]
    position = ring_position(members)
    chunks = grad_ref.shape[1] // (members * width)
    copies = []
    for i, d in enumerate(ways):
        start = pl.multiple_of((ring_owner(position, d, s, members) * chunks + j) * width, LANES)
        source = grad_ref.at[pl.ds(d * side, side), pl.ds(start, width)]
        copies.append(pltpu.make_async_copy(source, out_refs[i], sem_ref.at[i]))
        copies[-1].start()
    for copy in copies:
        copy.wait()


def stage_part(grad, ways, j, s, members, side, width):
    return pl.pallas_call(
        functools.partial(stage_kernel, members, side, j, s, ways),
        out_shape=[pltpu.VMEM((side, width), grad.dtype) for _ in ways],
        in_specs=[pl.BlockSpec(memory_space=pl.ANY)],
        out_specs=[ON_CHIP] * len(ways),
        scratch_shapes=[pltpu.SemaphoreType.DMA((len(ways),))],
        compiler_params=PARAMS,
        cost_estimate=cost(0, side * width * 4 * len(ways)),
    )(grad)


def join_kernel(arrived_ref, term_ref, out_ref):
    out_ref[...] = arrived_ref[...] + term_ref[...].astype(f32)


def join_part(arrived, term):
    return pl.pallas_call(
        join_kernel,
        out_shape=pltpu.VMEM(arrived.shape, f32),
        in_specs=[ON_CHIP] * 2,
        out_specs=ON_CHIP,
        compiler_params=PARAMS,
        cost_estimate=cost(arrived.size, arrived.size * 10),
    )(in_vmem(arrived), in_vmem(term))


def load_kernel(members, side, j, s, ways, grad_ref, *refs):
    out_refs, (buffer_ref, sem_ref) = refs[-2 - len(ways) : -2], refs[-2:]
    arrived_refs = refs[: -2 - len(ways)]
    width = out_refs[0].shape[1]
    position = ring_position(members)
    chunks = grad_ref.shape[1] // (members * width)
    copies = []
    for i, d in enumerate(ways):
        start = pl.multiple_of((ring_owner(position, d, s, members) * chunks + j) * width, LANES)
        source = grad_ref.at[pl.ds(d * side, side), pl.ds(start, width)]
        copies.append(pltpu.make_async_copy(source, buffer_ref.at[i], sem_ref.at[i]))
        copies[-1].start()
    for i, copy in enumerate(copies):
        copy.wait()
        term = buffer_ref[i].astype(f32)
        out_refs[i][...] = arrived_refs[i][...] + term if arrived_refs else term


def load_part(grad, arrived, ways, j, s, members, side, width):
    return pl.pallas_call(
        functools.partial(load_kernel, members, side, j, s, ways),
        out_shape=[pltpu.VMEM((side, width), f32) for _ in ways],
        in_specs=[pl.BlockSpec(memory_space=pl.ANY)] + [ON_CHIP] * len(arrived),
        out_specs=[ON_CHIP] * len(ways),
        scratch_shapes=[pltpu.VMEM((len(ways), side, width), grad.dtype), pltpu.SemaphoreType.DMA((len(ways),))],
        compiler_params=PARAMS,
        cost_estimate=cost(side * width, side * width * 6),
    )(grad, *[in_vmem(a) for a in arrived])


def ring_order(n):
    return [2 * q if q < n // 2 else 2 * n - 1 - 2 * q for q in range(n)]


CHUNKS = 2
HOPS = 3
LEAST_RING = HOPS + 5


def local(gradients, momentum, chosen, pods, members):
    kept = chosen.shape[3]
    side = GROUP
    per = LANES // kept
    span = per * side
    grad, mom = gradients[0, 0], momentum[0]
    rows, width = mom.shape
    blocks = rows // side
    pod = lax.axis_index("outer")

    basis = cosine_basis(side)
    many = np.kron(np.eye(per, dtype=np.float32), basis)
    wide, wide_t, tall = (jnp.asarray(parts_of(t)) for t in (many, many.T, basis.T))
    same = jnp.asarray(np.kron(np.eye(per), np.ones((side, side))).astype(bf16))
    how = dict(kept=kept, side=side)

    chunks = CHUNKS
    if blocks != 2 or members % 2 or members < LEAST_RING or width % (chunks * span):
        summed = lax.psum_scatter(grad.astype(f32), "dev", scatter_dimension=1, tiled=True)
        pad = -width % span
        mom, summed = (jnp.pad(a, ((0, 0), (0, pad))) for a in (mom, summed))
        places = jnp.pad(chosen, ((0, 0), (0, 0), (0, pad // side), (0, 0)))
        count = (width + pad) // span
        places = places.reshape(pods, blocks, count, 1, LANES)
        own_places = lax.dynamic_index_in_dim(places, pod, 0, keepdims=False)
        terms = [summed[r * side : (r + 1) * side] for r in range(blocks)]
        x, v = own_part(mom, terms, own_places, wide_t, tall, members=members, first=0, **how)
        tables = table_part(places, tall, **how)
        every = lax.all_gather(v, "outer")
        update, rest = decode_part(pod[None], every, tables, x, wide, same, side, 0, 1, None)
        return rest[None, :, :width], update[:, :width]

    count = width // span
    each = count // chunks
    piece_cols = width // chunks
    ring = ring_order(members)
    position = ring_position(members)

    def ahead(d, steps):
        move = steps if d == 0 else -steps
        return [(ring[i], ring[(i + move) % members]) for i in range(members)]

    def piece(source, d, s, j):
        start = ring_owner(position, d, s, members) * width + j * piece_cols
        return lax.dynamic_slice(source, (d * side, start), (side, piece_cols))

    def load(source, arrived, ways, j, s):
        return load_part(source, arrived, ways, j, s, members, side, piece_cols)

    def tie(*arrays):
        return lax.optimization_barrier(arrays)

    def spans(a, j):
        return a[..., j * each : (j + 1) * each, :, :]

    last = members - 2
    send = last + 1 - HOPS

    current = [[None] * 2 for _ in range(chunks)]
    token = ()
    for j in range(chunks):
        current[j] = list(load(tie(in_hbm(grad), *token)[0], (), (0, 1), j, 0))
        token = tuple(current[j])

    def after(array):
        return tie(array, *token)[0]

    second = [None] * chunks

    def stage(j):
        second[j] = stage_part(after(in_hbm(grad)), (0, 1), j, 1, members, side, piece_cols)
        return tuple(second[j])

    token = stage(0)

    def moved(both, steps):
        parts = []
        for d in range(2):
            parts.append(lax.ppermute(both[d], "dev", ahead(d, steps)))
        return jnp.stack(parts)

    places = after(chosen).reshape(pods, blocks, count, 1, LANES)
    own_places = lax.dynamic_index_in_dim(places, pod, 0, keepdims=False)
    near = [own_places]
    for _ in range(1, HOPS + 1):
        near.append(moved(near[-1], -1))
    near = near[1:]

    def terms(s, j):
        source = after(grad)
        return [piece(source, d, s, j) for d in range(2)]

    def own_filler(j):
        own[j] = own_part(
            mom,
            terms(members - 1, j),
            after(spans(own_places, j)),
            wide_t,
            tall,
            members=members,
            first=j * piece_cols,
            **how,
        )
        return own[j]

    def raw_filler(j):
        others = [t for steps in range(1, HOPS) for t in terms(members - 1 - steps, j)]
        where = jnp.concatenate([spans(p, j) for p in near[: HOPS - 1]], axis=0)
        raw[j] = term_part(others, after(where), wide_t, tall, members=members, **how)
        return (raw[j],)

    def sent_filler(j):
        sent[j] = term_part(current[j], after(spans(near[-1], j)), wide_t, tall, members=members, **how)
        return (sent[j],)

    def table_filler(j):
        tables[j] = table_part(after(spans(places, j)), tall, **how)
        return tables[j]

    own, raw, tables, sent = ([None] * chunks for _ in range(4))
    arrivals = [[None] * 2 for _ in range(chunks)]
    fillers = {send - 3: own_filler, send - 2: raw_filler, send - 1: sent_filler, send: table_filler}
    for s in range(members - 1):
        for j in range(chunks):
            for d in range(2):
                arrived = lax.ppermute(current[j][d], "dev", ahead(d, 1))
                if s < last:
                    arrived, source, *_ = tie(arrived, grad, *token)
                    if s == 0:
                        current[j][d] = join_part(arrived, second[j][d])
                    else:
                        current[j][d] = arrived + piece(source, d, s + 1, j).astype(f32)
                    token = (current[j][d],)
                else:
                    arrivals[j][d] = arrived
            if s == 0 and j + 1 < chunks:
                token += stage(j + 1)
            if s in fillers:
                token += tuple(fillers[s](j))
            if (s, j) == (send - 2, chunks - 1):
                both = jnp.concatenate(raw, axis=1)
                received = [moved(both[2 * n - 2 : 2 * n], n) for n in range(1, HOPS)]
            if (s, j) == (send - 1, chunks - 1):
                received.append(moved(jnp.concatenate(sent, axis=1), HOPS))
            if (s, j) == (send + 1, 0):
                values = jnp.concatenate([v for _, v in own], axis=1) + sum(received)
                every = lax.all_gather(after(values), "outer")
                token += (every,)
    update, rests = None, []
    for j in range(chunks):
        update, rest = decode_part(
            pod[None], after(every), tables[j], own[j][0], wide, same, side, j, chunks, update
        )
        rests.append(rest)
    out = None
    for j in range(chunks):
        out = finish_part(out, width, rests[j], arrivals[j], members, j * piece_cols)
    return out[None], update


def solution(mesh):
    def step(*args):
        return local(*args, pods=mesh.shape["outer"], members=mesh.shape["dev"])

    return jax.shard_map(
        step,
        mesh=mesh,
        in_specs=(
            P("outer", "dev", None, None),
            P("outer", None, "dev"),
            P(None, None, "dev", None),
        ),
        out_specs=(P("outer", None, "dev"), P(None, "dev")),
        check_vma=False,
    )
```

```python
import functools

import jax
import jax.numpy as jnp
import numpy as np
from jax import lax
from jax.experimental import pallas as pl
from jax.experimental.pallas import tpu as pltpu
from jax.sharding import PartitionSpec as P


GROUP = 64
LANES = 128

decay_rate = 0.999
tiny_eps = 1e-06


VMEM_LIMIT = 16 << 20
bf16 = jnp.bfloat16
f32 = jnp.float32


def cosine_basis(size):
    freq = np.arange(size, dtype=np.float64)[:, None]
    place = np.arange(size, dtype=np.float64)[None, :]
    weight = np.where(freq == 0, np.sqrt(1.0 / size), np.sqrt(2.0 / size))
    return (weight * np.cos(np.pi * (2.0 * place + 1.0) * freq / (2.0 * size))).astype(np.float32)


def parts_of(table):
    parts = []
    for _ in range(3):
        parts.append(table.astype(bf16))
        table = table - parts[-1].astype(np.float32)
    return np.stack(parts)


def split(x, count=3):
    parts = []
    for _ in range(count):
        parts.append(x.astype(bf16))
        x = x - parts[-1].astype(f32)
    return parts


def mm(a, b):
    return jnp.dot(a, b, preferred_element_type=f32)


def pick(x, one_hots, count=3):
    return sum(mm(part, one_hots) for part in reversed(split(x, count)))


def product(x, table):
    if x.dtype == bf16:
        return mm(x, table[0]) + (mm(x, table[1]) + mm(x, table[2]))
    high, middle, low = split(x)
    small = mm(low, table[0]) + (mm(middle, table[1]) + mm(high, table[2]))
    return mm(high, table[0]) + (mm(middle, table[0]) + (mm(high, table[1]) + small))


def log2(n):
    assert n & (n - 1) == 0
    return n.bit_length() - 1


def table_places(idx, kept, side):
    lane = lax.broadcasted_iota(jnp.int32, idx.shape, 1)
    cell = (lane & (LANES - 1)) >> log2(kept)
    return idx >> log2(side), (cell << log2(side)) + (idx & (side - 1))


def one_hot(hit):
    return jnp.where(hit, 1.0, 0.0).astype(bf16)


def basis_rows(row, tall, side):
    at_row = one_hot(lax.broadcasted_iota(jnp.int32, (side, row.shape[1]), 0) == row)
    return mm(tall[0], at_row) + (mm(tall[1], at_row) + mm(tall[2], at_row))


def picks_of(xs, places, wide_t, tall, kept, side):
    spectra = product(jnp.concatenate(xs, axis=0), wide_t)
    found = []
    for i, idx in enumerate(places):
        row, col = table_places(idx, kept, side)
        at_col = one_hot(lax.broadcasted_iota(jnp.int32, (spectra.shape[1], idx.shape[1]), 0) == col)
        cols = pick(spectra[i * side : (i + 1) * side], at_col)
        found.append(jnp.sum(cols * basis_rows(row, tall, side), axis=0, keepdims=True))
    return found


def in_hbm(a):
    return pltpu.with_memory_space_constraint(a, pltpu.HBM)


def in_vmem(a):
    return pltpu.with_memory_space_constraint(a, pltpu.VMEM)


ON_CHIP = pl.BlockSpec(memory_space=pltpu.VMEM)
PARAMS = pltpu.CompilerParams(vmem_limit_bytes=VMEM_LIMIT)


def cost(flops, moved):
    return pl.CostEstimate(flops=flops, bytes_accessed=moved, transcendentals=0)


def own_kernel(kept, side, members, first, mom_ref, *refs):
    *grad_refs, idx_ref, wide_t_ref, tall_ref, x_ref, v_ref = refs
    parts, count = idx_ref.shape[:2]
    span = wide_t_ref.shape[1]
    spots = [(r, q) for r in range(parts) for q in range(count)]
    xs = []
    for r, q in spots:
        rows = pl.ds(r * side, side)
        x = decay_rate * mom_ref[rows, pl.ds(first + q * span, span)]
        x += grad_refs[r][:, pl.ds(q * span, span)].astype(f32) / members
        x_ref[rows, pl.ds(q * span, span)] = x
        xs.append(x)
    places = [idx_ref[r, q] for r, q in spots]
    for (r, q), v in zip(spots, picks_of(xs, places, wide_t_ref, tall_ref, kept, side)):
        v_ref[r, q] = v


def own_part(mom, terms, idx, wide_t, tall, kept, side, members, first):
    shape = (mom.shape[0], terms[0].shape[1])
    size = shape[0] * shape[1]
    return pl.pallas_call(
        functools.partial(own_kernel, kept, side, members, first),
        out_shape=(pltpu.VMEM(shape, f32), jax.ShapeDtypeStruct(idx.shape, f32)),
        in_specs=[ON_CHIP] * (len(terms) + 4),
        out_specs=(ON_CHIP, ON_CHIP),
        compiler_params=PARAMS,
        cost_estimate=cost(size * wide_t.shape[1] * 10, size * 10),
    )(in_vmem(mom), *[in_vmem(x) for x in terms], idx, wide_t, tall)


def term_kernel(kept, side, members, *refs):
    *x_refs, idx_ref, wide_t_ref, tall_ref, v_ref = refs
    parts, count = idx_ref.shape[:2]
    span = wide_t_ref.shape[1]
    spots = [(r, q) for r in range(parts) for q in range(count)]
    xs = [x_refs[r][:, pl.ds(q * span, span)] for r, q in spots]
    places = [idx_ref[r, q] for r, q in spots]
    for (r, q), v in zip(spots, picks_of(xs, places, wide_t_ref, tall_ref, kept, side)):
        v_ref[r, q] = v / members


def term_part(terms, idx, wide_t, tall, kept, side, members):
    return pl.pallas_call(
        functools.partial(term_kernel, kept, side, members),
        out_shape=jax.ShapeDtypeStruct(idx.shape, f32),
        in_specs=[ON_CHIP] * (len(terms) + 3),
        out_specs=ON_CHIP,
        compiler_params=PARAMS,
        cost_estimate=cost(idx.size * side * wide_t.shape[1] * 40, idx.size * side * 4),
    )(*[in_vmem(x) for x in terms], idx, wide_t, tall)


def table_kernel(kept, side, idx_ref, tall_ref, rows_ref, cols_ref):
    pods, parts, count = idx_ref.shape[:3]
    span = cols_ref.shape[3]
    for r in range(parts):
        for q in range(count):
            idx = jnp.concatenate([idx_ref[p, r, q] for p in range(pods)], axis=1)
            row, col = table_places(idx, kept, side)
            rows_ref[r, q] = basis_rows(row, tall_ref, side)
            tall_col = jnp.transpose(jnp.broadcast_to(col, (LANES, col.shape[1])))
            for c in range(0, span, LANES):
                lane = lax.broadcasted_iota(jnp.int32, tall_col.shape, 1) + c
                cols_ref[r, q, :, pl.ds(c, LANES)] = one_hot(tall_col == lane)


def table_part(idx, tall, kept, side):
    pods, parts, count, _, lanes = idx.shape
    span = LANES // kept * side
    return pl.pallas_call(
        functools.partial(table_kernel, kept, side),
        out_shape=(
            pltpu.VMEM((parts, count, side, pods * lanes), f32),
            pltpu.VMEM((parts, count, pods * lanes, span), bf16),
        ),
        in_specs=[ON_CHIP] * 2,
        out_specs=(ON_CHIP, ON_CHIP),
        compiler_params=PARAMS,
        cost_estimate=cost(parts * count * side * side * pods * lanes * 4, parts * count * pods * lanes * span * 2),
    )(idx, tall)


def decode_kernel(side, chunk, v_ref, rows_ref, cols_ref, wide_ref, same_ref, *refs):
    update_hbm, table_ref, update_ref, sem_ref = refs[-4:]
    parts, count = rows_ref.shape[:2]
    pods, span = v_ref.shape[0], wide_ref.shape[1]
    for r in range(parts):
        for q in range(count):
            v = jnp.concatenate([v_ref[p, r, chunk * count + q] for p in range(pods)], axis=1)
            table_ref[r * count + q] = pick(rows_ref[r, q] * v, cols_ref[r, q])
    table = table_ref[...].reshape(parts * count * side, span)
    shared = product(table, wide_ref).reshape(parts * count, side, span)
    squares = jnp.sum(shared * shared, axis=1) / (side * side)
    scale = 1.0 / jnp.sqrt(pick(squares, same_ref[...]) + tiny_eps)
    for r in range(parts):
        for q in range(count):
            at, b = (pl.ds(r * side, side), pl.ds(q * span, span)), r * count + q
            update_ref[at] = shared[b] * scale[b : b + 1, :]
    columns = pl.ds(chunk * update_ref.shape[1], update_ref.shape[1])
    copy = pltpu.make_async_copy(update_ref, update_hbm.at[:, columns], sem_ref)
    copy.start()
    copy.wait()


def decode_part(values, tables, shape, wide, same, side, chunk, chunks, update):
    rows, cols = tables
    parts, count = rows.shape[:2]
    height, width = shape
    held = [] if update is None else [update]
    hbm = pl.BlockSpec(memory_space=pl.ANY)
    return pl.pallas_call(
        functools.partial(decode_kernel, side, chunk),
        out_shape=jax.ShapeDtypeStruct((height, chunks * width), f32),
        in_specs=[ON_CHIP] * 5 + [hbm] * len(held),
        out_specs=hbm,
        scratch_shapes=[
            pltpu.VMEM((parts * count, side, wide.shape[2]), f32),
            pltpu.VMEM(shape, f32),
            pltpu.SemaphoreType.DMA,
        ],
        input_output_aliases={5: 0} if held else {},
        compiler_params=PARAMS,
        cost_estimate=cost(height * width * wide.shape[2] * 16, height * width * 8),
    )(values, in_vmem(rows), in_vmem(cols), wide, same, *held)


def rest_kernel(side, v_ref, rows_ref, cols_ref, x_ref, wide_ref, rest_ref):
    parts, count = rows_ref.shape[:2]
    span = wide_ref.shape[1]
    spots = [(r, q) for r in range(parts) for q in range(count)]
    tables = [pick(rows_ref[r, q, :, :LANES] * v_ref[r, q], cols_ref[r, q, :LANES, :]) for r, q in spots]
    spatial = product(jnp.concatenate(tables, axis=0), wide_ref)
    for b, (r, q) in enumerate(spots):
        at = (pl.ds(r * side, side), pl.ds(q * span, span))
        rest_ref[at] = x_ref[at] - spatial[b * side : (b + 1) * side]


def rest_part(values, tables, x, wide, side):
    rows, cols = tables
    return pl.pallas_call(
        functools.partial(rest_kernel, side),
        out_shape=pltpu.VMEM(x.shape, f32),
        in_specs=[ON_CHIP] * 5,
        out_specs=ON_CHIP,
        compiler_params=PARAMS,
        cost_estimate=cost(x.size * wide.shape[2] * 10, x.size * 8),
    )(values, in_vmem(rows), in_vmem(cols), in_vmem(x), wide)


def finish_kernel(members, first, starts, rest_ref, *refs):
    arrived_refs, (out_ref, buffer_ref, sem_ref) = refs[: len(starts)], refs[-3:]
    height, width = arrived_refs[0].shape
    copies = []
    for d, arrived_ref in enumerate(arrived_refs):
        rows = pl.ds(starts[d], height)
        buffer_ref[rows, :] = rest_ref[rows, :] + arrived_ref[...] / members
        target = out_ref.at[rows, pl.ds(first, width)]
        copies.append(pltpu.make_async_copy(buffer_ref.at[rows], target, sem_ref.at[d]))
        copies[-1].start()
    for copy in copies:
        copy.wait()


def finish_part(out, columns, rest, arrived, members, first, starts):
    held = [] if out is None else [out]
    hbm = pl.BlockSpec(memory_space=pl.ANY)
    return pl.pallas_call(
        functools.partial(finish_kernel, members, first, starts),
        out_shape=jax.ShapeDtypeStruct((rest.shape[0], columns), f32),
        in_specs=[ON_CHIP] * (1 + len(arrived)) + [hbm] * len(held),
        out_specs=hbm,
        scratch_shapes=[pltpu.VMEM(rest.shape, f32), pltpu.SemaphoreType.DMA((len(arrived),))],
        input_output_aliases={1 + len(arrived): 0} if held else {},
        compiler_params=PARAMS,
        cost_estimate=cost(rest.size, rest.size * 12),
    )(in_vmem(rest), *[in_vmem(a) for a in arrived], *held)


def ring_position(members):
    me = lax.axis_index("dev")
    return jnp.where((me & 1) == 0, me >> 1, members - 1 - (me >> 1))


def ring_owner(position, d, s, members):
    q = position - 1 - s if d == 0 else position + 1 + s
    q = jnp.where(q < 0, q + members, jnp.where(q >= members, q - members, q))
    return jnp.where(q < members // 2, 2 * q, 2 * members - 1 - 2 * q)


def load_kernel(members, side, j, s, ways, grad_ref, *refs):
    out_refs, (buffer_ref, sem_ref) = refs[-2 - len(ways) : -2], refs[-2:]
    arrived_refs = refs[: -2 - len(ways)]
    width = out_refs[0].shape[1]
    position = ring_position(members)
    chunks = grad_ref.shape[1] // (members * width)
    copies = []
    for i, d in enumerate(ways):
        start = pl.multiple_of((ring_owner(position, d, s, members) * chunks + j) * width, LANES)
        source = grad_ref.at[pl.ds(d * side, side), pl.ds(start, width)]
        copies.append(pltpu.make_async_copy(source, buffer_ref.at[i], sem_ref.at[i]))
        copies[-1].start()
    for i, copy in enumerate(copies):
        copy.wait()
        term = buffer_ref[i].astype(f32)
        out_refs[i][...] = arrived_refs[i][...] + term if arrived_refs else term


def load_part(grad, arrived, ways, j, s, members, side, width):
    return pl.pallas_call(
        functools.partial(load_kernel, members, side, j, s, ways),
        out_shape=[pltpu.VMEM((side, width), f32) for _ in ways],
        in_specs=[pl.BlockSpec(memory_space=pl.ANY)] + [ON_CHIP] * len(arrived),
        out_specs=[ON_CHIP] * len(ways),
        scratch_shapes=[pltpu.VMEM((len(ways), side, width), grad.dtype), pltpu.SemaphoreType.DMA((len(ways),))],
        compiler_params=PARAMS,
        cost_estimate=cost(side * width, side * width * 6),
    )(grad, *[in_vmem(a) for a in arrived])


def ring_order(n):
    return [2 * q if q < n // 2 else 2 * n - 1 - 2 * q for q in range(n)]


CHUNKS = 2
STRIPS = 1
HOPS = 3
LEAST_RING = HOPS + 5


def local(gradients, momentum, chosen, pods, members):
    kept = chosen.shape[3]
    side = GROUP
    per = LANES // kept
    span = per * side
    grad, mom = gradients[0, 0], momentum[0]
    rows, width = mom.shape
    blocks = rows // side
    pod = lax.axis_index("outer")

    basis = cosine_basis(side)
    many = np.kron(np.eye(per, dtype=np.float32), basis)
    wide, wide_t, tall = (jnp.asarray(parts_of(t)) for t in (many, many.T, basis.T))
    same = jnp.asarray(np.kron(np.eye(per), np.ones((side, side))).astype(bf16))
    how = dict(kept=kept, side=side)

    chunks = CHUNKS
    if blocks != 2 or members % 2 or members < LEAST_RING or pods != 4 or width % (chunks * span):
        summed = lax.psum_scatter(grad.astype(f32), "dev", scatter_dimension=1, tiled=True)
        pad = -width % span
        mom, summed = (jnp.pad(a, ((0, 0), (0, pad))) for a in (mom, summed))
        places = jnp.pad(chosen, ((0, 0), (0, 0), (0, pad // side), (0, 0)))
        count = (width + pad) // span
        places = places.reshape(pods, blocks, count, 1, LANES)
        places = jnp.roll(places, -pod, axis=0)
        own_places = places[0]
        terms = [summed[r * side : (r + 1) * side] for r in range(blocks)]
        x, v = own_part(mom, terms, own_places, wide_t, tall, members=members, first=0, **how)
        tables = table_part(places, tall, **how)
        every = lax.all_gather(v, "outer")
        every = jnp.roll(every, -pod, axis=0)
        rest = rest_part(v, tables, x, wide, side)
        update = decode_part(every, tables, x.shape, wide, same, side, 0, 1, None)
        return rest[None, :, :width], update[:, :width]

    count = width // span
    each = count // chunks
    piece_cols = width // chunks
    ring = ring_order(members)
    position = ring_position(members)

    def ahead(d, steps):
        move = steps if d == 0 else -steps
        return [(ring[i], ring[(i + move) % members]) for i in range(members)]

    def piece(source, d, s, j):
        start = ring_owner(position, d, s, members) * width + j * piece_cols
        return lax.dynamic_slice(source, (d * side, start), (side, piece_cols))

    def load(source, arrived, ways, j, s):
        return load_part(source, arrived, ways, j, s, members, side, piece_cols)

    def tie(*arrays):
        return lax.optimization_barrier(arrays)

    def spans(a, j):
        return a[..., j * each : (j + 1) * each, :, :]

    last = members - 2
    send = last + 1 - HOPS

    current = [[None] * 2 for _ in range(chunks)]
    token = ()
    for j in range(chunks):
        current[j] = list(load(tie(in_hbm(grad), *token)[0], (), (0, 1), j, 0))
        token = tuple(current[j])

    def after(array):
        return tie(array, *token)[0]

    def moved(both, steps):
        parts = []
        for d in range(2):
            parts.append(lax.ppermute(both[d], "dev", ahead(d, steps)))
        return jnp.stack(parts)

    places = after(chosen).reshape(pods, blocks, count, 1, LANES)
    places = jnp.concatenate([lax.dynamic_slice_in_dim(places, pod ^ i, 1, 0) for i in range(pods)], axis=0)
    own_places = places[0]
    near = [own_places]
    for _ in range(1, HOPS + 1):
        near.append(moved(near[-1], -1))
    near = near[1:]

    def terms(s, j):
        source = after(grad)
        return [piece(source, d, s, j) for d in range(2)]

    def own_filler(j):
        own[j] = own_part(
            mom,
            terms(members - 1, j),
            after(spans(own_places, j)),
            wide_t,
            tall,
            members=members,
            first=j * piece_cols,
            **how,
        )
        return own[j]

    def raw_filler(j):
        others = [t for steps in range(1, HOPS) for t in terms(members - 1 - steps, j)]
        where = jnp.concatenate([spans(p, j) for p in near[: HOPS - 1]], axis=0)
        raw[j] = term_part(others, after(where), wide_t, tall, members=members, **how)
        return (raw[j],)

    def sent_filler(j):
        sent[j] = term_part(current[j], after(spans(near[-1], j)), wide_t, tall, members=members, **how)
        return (sent[j],)

    def table_filler(j):
        tables[j] = table_part(after(spans(places, j)), tall, **how)
        return tables[j]

    own, raw, tables, sent = ([None] * chunks for _ in range(4))
    arrivals = [[None] * 2 for _ in range(chunks)]
    fillers = {send - 3: own_filler, send - 2: raw_filler, send - 1: sent_filler}
    fillers = {(s, j): (fill, j) for s, fill in fillers.items() for j in range(chunks)}
    fillers |= {(send, j): (table_filler, j) for j in range(chunks)}
    rests = [None] * chunks

    def rest_filler(_):
        for j in range(chunks):
            rests[j] = rest_part(after(spans(every[0], j)), tables[j], own[j][0], wide, side)
        return rests

    fillers[send + 1, 0] = (rest_filler, None)
    for s in range(members - 1):
        for j in range(chunks):
            for d in range(2):
                strips = STRIPS if (s, j) == (last, chunks - 1) else 1
                arrived = [lax.ppermute(a, "dev", ahead(d, 1)) for a in jnp.split(current[j][d], strips)]
                if s < last:
                    arrived, source, *_ = tie(arrived[0], grad, *token)
                    if s == 0:
                        (current[j][d],) = load(in_hbm(source), (arrived,), (d,), j, s + 1)
                    else:
                        current[j][d] = arrived + piece(source, d, s + 1, j).astype(f32)
                    token = (current[j][d],)
                else:
                    arrivals[j][d] = arrived
            if (s, j) == (send, chunks - 1):
                every = (jnp.concatenate([v for _, v in own], axis=1) + sum(received))[None]
                exchange = [1 << i for i in range(log2(pods))]
            if (s, j) >= (send, chunks - 1) and s <= send + 1 and exchange:
                bit = exchange.pop(0)
                other = lax.ppermute(after(every), "outer", [(i, i ^ bit) for i in range(pods)])
                every = jnp.concatenate([every, other], axis=0)
            if (s, j) in fillers:
                fill, i = fillers[s, j]
                token += tuple(fill(i))
            if (s, j) == (send - 2, chunks - 1):
                both = jnp.concatenate(raw, axis=1)
                received = [moved(both[2 * n - 2 : 2 * n], n) for n in range(1, HOPS)]
            if (s, j) == (send - 1, chunks - 1):
                received.append(moved(jnp.concatenate(sent, axis=1), HOPS))
    assert not exchange
    update = None
    for j in range(chunks):
        update = decode_part(
            after(every), tables[j], own[j][0].shape, wide, same, side, j, chunks, update
        )
    out = None
    for j in range(chunks):
        strips = 1 if j < chunks - 1 else STRIPS
        for k in range(strips):
            arrived = [arrivals[j][d][k] for d in range(2)]
            starts = [d * side + k * (side // strips) for d in range(2)]
            out = finish_part(out, width, rests[j], arrived, members, j * piece_cols, starts)
    return out[None], update


def solution(mesh):
    def step(*args):
        return local(*args, pods=mesh.shape["outer"], members=mesh.shape["dev"])

    return jax.shard_map(
        step,
        mesh=mesh,
        in_specs=(
            P("outer", "dev", None, None),
            P("outer", None, "dev"),
            P(None, None, "dev", None),
        ),
        out_specs=(P("outer", None, "dev"), P(None, "dev")),
        check_vma=False,
    )
```
